128 devices in a mesh: gx: 16 (over x, z_hi, core), gy: 8 (over z_lo, y).
Axes of the slice: x: 4, y: 4, z: 4 (z_hi: 2, z_lo: 2; z = z_hi * 2 + z_lo), core: 2. Of those that a mesh axis runs over, the one named last changes fastest.
Arguments:
- volume: bfloat16 [64, 32, 128, 128], P(None, 'gx', 'gy'), may hold values from -6 to 6
- kernel: bfloat16 [4, 4, 4, 32, 64], replicated, may hold values from -0.25 to 0.25
- cotangent: bfloat16 [2, 2, 2, 32, 32, 128, 128], P(None, None, None, None, 'gx', 'gy'), may hold values from -6 to 6
Outputs:
- activation: bfloat16 [2, 2, 2, 32, 32, 128, 128], P(None, None, None, None, 'gx', 'gy')
- input_grad: bfloat16 [64, 32, 128, 128], P(None, 'gx', 'gy')
- weight_grad: float32 [4, 4, 4, 32, 64], replicated
The draws below stay inside these ranges and needn't reach their ends.
All inputs are finite; a program needn't handle non-finite values.
Results may differ from the reference program's by a relative error of at most 0.0049.
Values may be sent and summed in bfloat16 or wider, within the bound.
A program may use at most 192 MiB of HBM per device.

```python
import math
import jax
import jax.numpy as jnp

CI = 64
CO = 32
K = 4
NZ = 128
NX = 32
NY = 128


def levels(key, extent, split, least, top_value):
    level, own = 1.0, jax.random.fold_in(key, 6)
    for position, blocks in split:
        steps = jnp.exp(jax.random.uniform(jax.random.fold_in(own, position), (blocks,), jnp.float32, least / len(split), top_value / len(split)))
        level = level * jnp.repeat(steps, extent[position] // blocks).reshape([-1 if axis == position else 1 for axis in range(len(extent))])
    return level


def scatter_about(own_key, dims, scale, bound, pieces=(), dtype=jnp.bfloat16):
    result = scale * jax.random.normal(own_key, dims, jnp.float32)
    if pieces:
        result = result * levels(own_key, dims, pieces, -0.22, 0.18)
    return jnp.clip(result, -bound, bound).astype(dtype)


def setup_inputs(seed: int = 0) -> dict:
    key_list = jax.random.split(jax.random.key(seed), 4)
    return {
        "volume": scatter_about(key_list[0], (CI, NX, NY, NZ), 1.0, 6.0, ((1, 16), (2, 8))),
        "kernel": scatter_about(key_list[1], (K, K, K, CO, CI), (8 * CI) ** -0.5, 0.25),
        "cotangent": scatter_about(key_list[2], (2, 2, 2, CO, NX, NY, NZ), 1.0, 6.0, ((4, 16), (5, 8))),
    }


FORWARD_TAPS = (((1, 0), (3, -1)), ((2, 0), (0, 1)))
BACK_TAPS = ((1, -1), (0, 0), (1, 0), (0, 1))

def silu_pair(before):
    sigmoid = jax.nn.sigmoid(before)
    return (before * sigmoid, sigmoid * (1.0 + before * (1.0 - sigmoid)))

def reference(volume, kernel, cotangent):
    cells = NX * NY * NZ
    padded = jnp.pad(volume, ((0, 0), (1, 1), (1, 1), (1, 1)))
    act_phases = []
    grad_phases = []
    for phase_x in range(2):
        for phase_y in range(2):
            for phase_z in range(2):
                running = jnp.zeros((CO, cells), jnp.float32)
                for tap_x, shift_x in FORWARD_TAPS[phase_x]:
                    for tap_y, shift_y in FORWARD_TAPS[phase_y]:
                        for tap_z, shift_z in FORWARD_TAPS[phase_z]:
                            sliced = padded[:, 1 + shift_x:1 + shift_x + NX, 1 + shift_y:1 + shift_y + NY, 1 + shift_z:1 + shift_z + NZ].reshape(CI, cells)
                            running = running + jnp.dot(kernel[tap_x, tap_y, tap_z], sliced, preferred_element_type=jnp.float32)
                values, slopes = silu_pair(running)
                act_phases.append(values.astype(jnp.bfloat16).reshape(CO, NX, NY, NZ))
                cot_phase = cotangent[phase_x, phase_y, phase_z].reshape(CO, cells)
                grad_phase = (cot_phase.astype(jnp.float32) * slopes).astype(jnp.bfloat16)
                grad_phases.append(jnp.pad(grad_phase.reshape(CO, NX, NY, NZ), ((0, 0), (1, 1), (1, 1), (1, 1))))
    activation = jnp.stack(act_phases).reshape(2, 2, 2, CO, NX, NY, NZ)
    flat_volume = volume.reshape(CI, cells)
    back_sum = jnp.zeros((CI, cells), jnp.float32)
    weight_parts = []
    for tap_x in range(K):
        for tap_y in range(K):
            for tap_z in range(K):
                phase_x, shift_x = BACK_TAPS[tap_x]
                phase_y, shift_y = BACK_TAPS[tap_y]
                phase_z, shift_z = BACK_TAPS[tap_z]
                source = grad_phases[4 * phase_x + 2 * phase_y + phase_z]
                sliced = source[:, 1 + shift_x:1 + shift_x + NX, 1 + shift_y:1 + shift_y + NY, 1 + shift_z:1 + shift_z + NZ].reshape(CO, cells)
                back_sum = back_sum + jnp.dot(kernel[tap_x, tap_y, tap_z].T, sliced, preferred_element_type=jnp.float32)
                weight_parts.append(jnp.dot(sliced, flat_volume.T, preferred_element_type=jnp.float32))
    scaling = 1.0 / math.sqrt(NX * NY * NZ)
    weight_grad = jnp.stack(weight_parts).reshape(K, K, K, CO, CI) * scaling
    input_grad = back_sum.astype(jnp.bfloat16).reshape(CI, NX, NY, NZ)
    return (activation, input_grad, weight_grad)
```

```python
import functools
import math

import jax
import jax.numpy as jnp
from jax import lax
from jax.experimental import pallas as pl
from jax.experimental.pallas import tpu as pltpu
from jax.sharding import PartitionSpec as P

BF = jnp.bfloat16
F32 = jnp.float32
MESH = pl.DeviceIdType.MESH
BACK = ((1, -1), (0, 0), (1, 0), (0, 1))
ROWS = 16
WIDE = ROWS * 128
HALO = (ROWS + 2) * 128


def remote(src, dst, send, recv, device):
    return pltpu.make_async_remote_copy(
        src_ref=src, dst_ref=dst, send_sem=send, recv_sem=recv,
        device_id=device, device_id_type=MESH,
    )


def nt_dot(a, b):
    return lax.dot_general(a, b, (((1,), (1,)), ((), ())), preferred_element_type=F32)


def lanes(start, size):
    return pl.ds(pl.multiple_of(start, 128), size)


def step_kernel(
    scaling, vol_ref, ker_ref, cot_ref, act_ref, ig_ref, wg_ref,
    volb, face, turn, vt, cotb, cotf, actf, actb, g_s, ak, bk, w_s,
    w_send, w_recv, w_bf, rs_in, part, z_in, fin,
    igf, igb, igy, rx, ry, rc, igo, wgo,
    l_sem, o_sem, fs, fr, bs, br, ws, wr,
):
    gx, gy = lax.axis_index("gx"), lax.axis_index("gy")
    core = lax.rem(gx, 2)
    x, z_hi = gx // 4, lax.rem(gx // 2, 2)
    z_lo, y = gy // 4, lax.rem(gy, 4)
    z = 2 * z_hi + z_lo
    other = 1 - core
    far_gx = lax.rem(gx + 15 + 2 * core, 16)
    sib_gx = gx + 1 - 2 * core
    low_gy, high_gy = lax.rem(gy + 7, 8), lax.rem(gy + 1, 8)
    first_y, last_y = gy == 0, gy == 7
    no_far = jnp.logical_or(gx == 0, gx == 15)

    def plane_peer(i):
        px, py = lax.rem(x + i // 4, 4), lax.rem(y + i % 4, 4)
        return px * 4 + py, (px * 4 + 2 * z_hi + core, 4 * z_lo + py)

    def z_peer(i):
        pz = lax.rem(z + i, 4)
        return (4 * x + 2 * (pz // 2) + core, 4 * lax.rem(pz, 2) + y)

    neighbours = [
        (far_gx, gy), (sib_gx, gy), (gx, low_gy), (gx, high_gy),
        (far_gx, low_gy), (far_gx, high_gy), (sib_gx, low_gy), (sib_gx, high_gy),
    ]
    peers = neighbours + [plane_peer(i)[1] for i in range(1, 16)] + [z_peer(i) for i in range(1, 4)]

    vol_copy = pltpu.make_async_copy(vol_ref, volb, l_sem.at[4])
    vol_copy.start()
    blocks = [(1, 0), (0, 1), (other, other), (core, core)]
    cot_copies = []
    for k, (p, m) in enumerate(blocks):
        copy = pltpu.make_async_copy(
            cot_ref.at[pl.ds(4 * p, 4), :, m], cotb.at[k], l_sem.at[k]
        )
        copy.start()
        cot_copies.append(copy)

    barrier = pltpu.get_barrier_semaphore()
    for peer in peers:
        pl.semaphore_signal(barrier, inc=1, device_id=peer, device_id_type=MESH)

    for p in range(2):
        for q in range(2):
            pieces = [
                ker_ref[a, b].reshape(128, 64)
                for a in (1 + p, 3 - 3 * p)
                for b in (1 + q, 3 - 3 * q)
            ]
            ak[p, q] = jnp.concatenate(pieces, axis=1)
    for a in range(4):
        bk[a] = ker_ref[a].reshape(512, 64).astype(F32).T.astype(BF)
    g_s[:, :, :, :, 0:256] = jnp.zeros((2, 2, 2, 128, 256), BF)
    g_s[:, :, :, :, 256 + WIDE:] = jnp.zeros((2, 2, 2, 128, 256), BF)

    vol_copy.wait()
    pl.semaphore_wait(barrier, len(peers))

    sends = [
        remote(volb.at[:, core], face.at[0], fs.at[0], fr.at[0], neighbours[0]),
        remote(volb.at[:, other], face.at[1], fs.at[1], fr.at[1], neighbours[1]),
    ]
    for copy in sends:
        copy.start()

    def turn_in(get, slot):
        turn[...] = get().astype(F32).reshape(64 * ROWS, 128)

        def row(n, _):
            vt[slot, :, lanes((n + 1) * 128, 128)] = turn[pl.ds(n, 64, stride=ROWS), :].astype(BF)
            return 0

        lax.fori_loop(0, ROWS, row, 0, unroll=True)

    turn_in(lambda: volb[:, 0], 1)
    turn_in(lambda: volb[:, 1], 2)

    first, last = pl.ds(128, 128), pl.ds(ROWS * 128, 128)
    low, high = pl.ds(0, 128), pl.ds((ROWS + 1) * 128, 128)
    own = pl.ds(1, 2)
    ysends = [
        remote(vt.at[own, :, first], vt.at[own, :, high], fs.at[2], fr.at[2], neighbours[2]),
        remote(vt.at[own, :, last], vt.at[own, :, low], fs.at[3], fr.at[3], neighbours[3]),
    ]
    for k, (m, slot) in enumerate(((core, 3 - 3 * core), (other, 3 * core))):
        base = 4 + 2 * k
        ysends.append(remote(vt.at[1 + m, :, first], vt.at[slot, :, high], fs.at[base], fr.at[base], neighbours[base]))
        ysends.append(remote(vt.at[1 + m, :, last], vt.at[slot, :, low], fs.at[base + 1], fr.at[base + 1], neighbours[base + 1]))
    for copy in ysends:
        copy.start()
    sends += ysends

    lane = lax.broadcasted_iota(jnp.int32, (32, 128), 1)

    def up(u):
        return jnp.where(lane == 0, 0.0, pltpu.roll(u, 1, axis=1))

    def down(u):
        return jnp.where(lane == 127, 0.0, pltpu.roll(u, 127, axis=1))

    def stacked(near, far, q, start, size):
        shift = 2 * q
        return jnp.concatenate(
            [
                vt[near, :, lanes(start + 128, size)],
                vt[near, :, lanes(start + 128 * shift, size)],
                vt[far, :, lanes(start + 128, size)],
                vt[far, :, lanes(start + 128 * shift, size)],
            ],
            axis=0,
        )

    def block(k):
        p, m = blocks[k]
        near, far = m + 1, m + 2 * p
        cot_copies[k].wait()
        cotf[...] = cotb[k].astype(F32).reshape(4 * 32 * ROWS, 128)
        for q in range(2):

            def chunk(ci, _):
                u = jnp.dot(
                    ak[p, q], stacked(near, far, q, ci * 512, 512), preferred_element_type=F32
                )
                for j in range(4):
                    n = ci * 4 + j
                    taps = [u[32 * c:32 * c + 32, 128 * j:128 * j + 128] for c in range(4)]
                    pre = (taps[1] + up(taps[3]), taps[2] + down(taps[0]))
                    grads = []
                    for s in range(2):
                        rows = pl.ds((2 * q + s) * 32 * ROWS + n, 32, stride=ROWS)
                        sig = 0.5 * jnp.tanh(0.5 * pre[s]) + 0.5
                        act = pre[s] * sig
                        actf[rows, :] = act
                        grads.append(cotf[rows, :] * (sig + act * (1.0 - sig)))
                    four = (up(grads[1]), grads[0], grads[1], down(grads[0]))
                    g_s[p, q, m, :, lanes((n + 2) * 128, 128)] = jnp.concatenate(
                        [value.astype(BF) for value in four], axis=0
                    )
                return 0

            lax.fori_loop(0, ROWS // 4, chunk, 0)

            def grad(ci, total):
                return total + nt_dot(
                    g_s[p, q, m, :, lanes((2 + 4 * ci) * 128, 512)],
                    stacked(near, far, q, ci * 512, 512),
                )

            start = jnp.zeros((128, 256), F32) if k < 2 else w_s[p, q]
            w_s[p, q] = lax.fori_loop(0, ROWS // 4, grad, start)
        actb[k] = actf[...].reshape(4, 32, ROWS, 128).astype(BF)
        copy = pltpu.make_async_copy(actb.at[k], act_ref.at[pl.ds(4 * p, 4), :, m], o_sem.at[k])
        copy.start()
        return copy

    ysends[0].wait_recv()
    ysends[1].wait_recv()

    @pl.when(first_y)
    def _():
        vt[own, :, low] = jnp.zeros((2, 64, 128), BF)

    @pl.when(last_y)
    def _():
        vt[own, :, high] = jnp.zeros((2, 64, 128), BF)

    outs = [block(0), block(1)]

    def halo(index, slot):
        sends[index].wait_recv()
        turn_in(lambda: face[index], slot)
        sends[4 + 2 * index].wait_recv()
        sends[5 + 2 * index].wait_recv()

        @pl.when(first_y)
        def _():
            vt[slot, :, low] = jnp.zeros((64, 128), BF)

        @pl.when(last_y)
        def _():
            vt[slot, :, high] = jnp.zeros((64, 128), BF)

    halo(1, 3 - 3 * core)
    outs.append(block(2))
    w_send[...] = w_s[other].reshape(256, 256).astype(BF)
    swap = remote(w_send, w_recv, ws.at[0], wr.at[0], neighbours[1])
    swap.start()

    halo(0, 3 * core)

    @pl.when(no_far)
    def _():
        vt[3 * core] = jnp.zeros((64, HALO), BF)

    outs.append(block(3))

    swap.wait_recv()
    w_s[core] = w_s[core] + w_recv[...].astype(F32).reshape(2, 128, 256)
    w_bf[...] = w_s[core].reshape(256, 256).astype(BF)
    scatter = []
    for i in range(1, 16):
        index, peer = plane_peer(i)
        scatter.append(remote(w_bf.at[pl.ds(pl.multiple_of(16 * index, 16), 16)], rs_in.at[i], ws.at[1], wr.at[1], peer))
    for copy in scatter:
        copy.start()

    def back(target, terms, ci):
        total = None
        for a, p, m in terms:
            parts = [
                g_s[p, BACK[b][0], m, :, lanes((ci * 6 + 1 + BACK[b][1]) * 128, 768)]
                for b in range(4)
            ]
            product = jnp.dot(bk[a], jnp.concatenate(parts, axis=0), preferred_element_type=F32)
            total = product if total is None else total + product
        return total

    def outer(ci, _):
        igb[0, :, lanes(ci * 768, 768)] = back(0, ((3, 0, 0),), ci).astype(BF)
        igb[1, :, lanes(ci * 768, 768)] = back(3, ((0, 1, 1),), ci).astype(BF)
        return 0

    lax.fori_loop(0, 3, outer, 0)
    body = pl.ds(128, WIDE)
    bsends = [
        remote(igb.at[core, :, body], rx.at[0], bs.at[0], br.at[0], neighbours[0]),
        remote(igb.at[other, :, body], rx.at[1], bs.at[1], br.at[1], neighbours[1]),
    ]
    for copy in bsends:
        copy.start()

    def inner(ci, _):
        igf[0, :, lanes(ci * 768, 768)] = back(1, ((1, 0, 0), (2, 1, 0), (3, 0, 1)), ci)
        igf[1, :, lanes(ci * 768, 768)] = back(2, ((1, 0, 1), (2, 1, 1), (0, 1, 0)), ci)
        return 0

    lax.fori_loop(0, 3, inner, 0)
    igy[0] = igf[:, :, 0:128].astype(BF)
    igy[1] = igf[:, :, HALO - 128:].astype(BF)
    for k in range(2):
        bsends.append(remote(igy.at[k], ry.at[k], bs.at[2 + k], br.at[2 + k], neighbours[2 + k]))
    for index, m in ((0, core), (1, other)):
        for k, part_lanes in enumerate((low, high)):
            at = 4 + 2 * index + k
            bsends.append(remote(igb.at[m, :, part_lanes], rc.at[index, k], bs.at[at], br.at[at], neighbours[at]))
    for copy in bsends[2:]:
        copy.start()

    mine = 4 * x + y
    remote(w_bf.at[pl.ds(0, 240)].reshape(15, 16, 256), rs_in.at[pl.ds(1, 15)], ws.at[1], wr.at[1], neighbours[1]).wait_recv()
    q = mine // 8
    total = w_s[core, q, pl.ds(pl.multiple_of(16 * lax.rem(mine, 8), 16), 16)]
    for i in range(1, 16):
        total = total + rs_in[i].astype(F32)
    part[...] = total
    z_in[z] = total
    gather_z = [remote(part, z_in.at[z], ws.at[2], wr.at[2], z_peer(i)) for i in range(1, 4)]
    for copy in gather_z:
        copy.start()
    three = z_in.at[pl.ds(0, 3)]
    remote(three, three, ws.at[2], wr.at[2], neighbours[1]).wait_recv()
    total = (z_in[0] + z_in[1]) + (z_in[2] + z_in[3])
    fin[core, pl.ds(pl.multiple_of(16 * mine, 16), 16)] = (total * scaling).astype(BF)
    spread = []
    for i in range(1, 16):
        _, peer = plane_peer(i)
        shard = fin.at[core, pl.ds(pl.multiple_of(16 * mine, 16), 16)]
        spread.append(remote(shard, shard, ws.at[3], wr.at[3], peer))
    for copy in spread:
        copy.start()

    def add(index, k, src, m, keep):
        place = (128, ROWS * 128)[k]

        @pl.when(keep)
        def _():
            igf[m, :, pl.ds(place, 128)] = igf[m, :, pl.ds(place, 128)] + src().astype(F32)

    bsends[2].wait_recv()
    bsends[3].wait_recv()
    for m in range(2):
        add(2, 1, lambda m=m: ry[0, m], m, jnp.logical_not(last_y))
        add(3, 0, lambda m=m: ry[1, m], m, jnp.logical_not(first_y))
    for index, m in ((1, other), (0, core)):
        ok = jnp.logical_not(no_far) if index == 0 else True
        bsends[index].wait_recv()
        bsends[4 + 2 * index].wait_recv()
        bsends[5 + 2 * index].wait_recv()

        def add_face(index=index, m=m):
            igf[m, :, body] = igf[m, :, body] + rx[index].astype(F32)

        if index == 0:
            pl.when(ok)(add_face)
        else:
            add_face()
        add(4, 1, lambda index=index: rc[index, 0], m, jnp.logical_and(ok, jnp.logical_not(last_y)))
        add(5, 0, lambda index=index: rc[index, 1], m, jnp.logical_and(ok, jnp.logical_not(first_y)))
        for n in range(ROWS):
            turn[pl.ds(n, 64, stride=ROWS), :] = igf[m, :, pl.ds((n + 1) * 128, 128)]
        igo[:, m] = turn[...].reshape(64, ROWS, 128).astype(BF)
    ig_copy = pltpu.make_async_copy(igo, ig_ref, o_sem.at[4])
    ig_copy.start()
    outs.append(ig_copy)

    remote(w_bf.at[pl.ds(0, 240)], fin.at[core, pl.ds(0, 240)], ws.at[3], wr.at[3], neighbours[1]).wait_recv()
    both = remote(fin.at[core], fin.at[core], ws.at[4], wr.at[4], neighbours[1])
    both.start()
    both.wait_recv()
    for p in range(2):
        for q in range(2):
            for i, (a, b) in enumerate([(a, b) for a in (1 + p, 3 - 3 * p) for b in (1 + q, 3 - 3 * q)]):
                value = fin[p, 128 * q:128 * q + 128, 64 * i:64 * i + 64]
                wgo[a, b] = value.astype(F32).reshape(4, 32, 64)
    wg_copy = pltpu.make_async_copy(wgo, wg_ref, o_sem.at[5])
    wg_copy.start()
    outs.append(wg_copy)

    for copy in sends + bsends + [swap, both]:
        copy.wait_send()
    remote(three, three, ws.at[2], wr.at[2], neighbours[1]).wait_send()
    remote(w_bf.at[pl.ds(0, 240)], fin.at[core, pl.ds(0, 240)], ws.at[1], wr.at[1], neighbours[1]).wait_send()
    remote(w_bf.at[pl.ds(0, 240)], fin.at[core, pl.ds(0, 240)], ws.at[3], wr.at[3], neighbours[1]).wait_send()
    for copy in outs:
        copy.wait()


def on_device(volume, kernel, cotangent):
    cells = volume.shape[1] * volume.shape[2] * volume.shape[3]
    scaling = 1.0 / math.sqrt(cells * lax.axis_size("gx") * lax.axis_size("gy"))
    anywhere = pl.BlockSpec(memory_space=pl.ANY)
    inside = pl.BlockSpec(memory_space=pltpu.VMEM)
    dma = pltpu.SemaphoreType.DMA
    act, ig, wg = pl.pallas_call(
        functools.partial(step_kernel, scaling),
        out_shape=(
            jax.ShapeDtypeStruct((8, 32, 2, ROWS, 128), BF),
            jax.ShapeDtypeStruct((64, 2, ROWS, 128), BF),
            jax.ShapeDtypeStruct((4, 4, 4, 32, 64), F32),
        ),
        in_specs=[anywhere, inside, anywhere],
        out_specs=(anywhere, anywhere, anywhere),
        scratch_shapes=[
            pltpu.VMEM((64, 2, ROWS, 128), BF),
            pltpu.VMEM((2, 64, ROWS, 128), BF),
            pltpu.VMEM((64 * ROWS, 128), F32),
            pltpu.VMEM((4, 64, HALO), BF),
            pltpu.VMEM((4, 4, 32, ROWS, 128), BF),
            pltpu.VMEM((4 * 32 * ROWS, 128), F32),
            pltpu.VMEM((4 * 32 * ROWS, 128), F32),
            pltpu.VMEM((4, 4, 32, ROWS, 128), BF),
            pltpu.VMEM((2, 2, 2, 128, (ROWS + 4) * 128), BF),
            pltpu.VMEM((2, 2, 128, 256), BF),
            pltpu.VMEM((4, 64, 512), BF),
            pltpu.VMEM((2, 2, 128, 256), F32),
            pltpu.VMEM((256, 256), BF),
            pltpu.VMEM((256, 256), BF),
            pltpu.VMEM((256, 256), BF),
            pltpu.VMEM((16, 16, 256), BF),
            pltpu.VMEM((16, 256), F32),
            pltpu.VMEM((4, 16, 256), F32),
            pltpu.VMEM((2, 256, 256), BF),
            pltpu.VMEM((2, 64, HALO), F32),
            pltpu.VMEM((2, 64, HALO), BF),
            pltpu.VMEM((2, 2, 64, 128), BF),
            pltpu.VMEM((2, 64, WIDE), BF),
            pltpu.VMEM((2, 2, 64, 128), BF),
            pltpu.VMEM((2, 2, 64, 128), BF),
            pltpu.VMEM((64, 2, ROWS, 128), BF),
            pltpu.VMEM((4, 4, 4, 32, 64), F32),
            dma((5,)), dma((6,)), dma((8,)), dma((8,)), dma((8,)), dma((8,)), dma((5,)), dma((5,)),
        ],
        compiler_params=pltpu.CompilerParams(
            collective_id=0, has_side_effects=True, vmem_limit_bytes=60 * 1024 * 1024
        ),
        name="conv_step",
    )(volume, kernel, cotangent.reshape(8, 32, 2, ROWS, 128))
    return act.reshape(2, 2, 2, 32, 2, ROWS, 128), ig, wg


def solution(mesh):
    placed = (P(None, "gx", "gy", None), P(), P(None, None, None, None, "gx", "gy", None))
    return jax.shard_map(
        on_device,
        mesh=mesh,
        in_specs=placed,
        out_specs=(P(None, None, None, None, "gx", "gy", None), P(None, "gx", "gy", None), P()),
        check_vma=False,
    )
```

```python
import functools
import math

import jax
import jax.numpy as jnp
from jax import lax
from jax.experimental import pallas as pl
from jax.experimental.pallas import tpu as pltpu
from jax.sharding import PartitionSpec as P

BF = jnp.bfloat16
F32 = jnp.float32
MESH = pl.DeviceIdType.MESH
BACK = ((1, -1), (0, 0), (1, 0), (0, 1))
ROWS = 16
WIDE = ROWS * 128
HALO = (ROWS + 2) * 128


def remote(src, dst, send, recv, device):
    return pltpu.make_async_remote_copy(
        src_ref=src, dst_ref=dst, send_sem=send, recv_sem=recv,
        device_id=device, device_id_type=MESH,
    )


def nt_dot(a, b):
    return lax.dot_general(a, b, (((1,), (1,)), ((), ())), preferred_element_type=F32)


def lanes(start, size):
    return pl.ds(pl.multiple_of(start, 128), size)


def step_kernel(
    scaling, vol_ref, ker_hbm, cot_ref, act_ref, igo, fin,
    volb, ker_ref, face, turn, vt, cotb, cotf, actf, ua, ub, g_s, ak, bk, w_s,
    w_send, w_recv, w_bf, rs_in, part, z_in,
    igf, igb, igy, rx, ry, rc,
    l_sem, fs, fr, bs, br, ws, wr,
):
    gx, gy = lax.axis_index("gx"), lax.axis_index("gy")
    core = lax.rem(gx, 2)
    x, z_hi = gx // 4, lax.rem(gx // 2, 2)
    z_lo, y = gy // 4, lax.rem(gy, 4)
    z = 2 * z_hi + z_lo
    other = 1 - core
    far_gx = lax.rem(gx + 15 + 2 * core, 16)
    sib_gx = gx + 1 - 2 * core
    low_gy, high_gy = lax.rem(gy + 7, 8), lax.rem(gy + 1, 8)
    first_y, last_y = gy == 0, gy == 7
    no_far = jnp.logical_or(gx == 0, gx == 15)

    def plane_peer(i):
        px, py = lax.rem(x + i // 4, 4), lax.rem(y + i % 4, 4)
        return px * 4 + py, (px * 4 + 2 * z_hi + core, 4 * z_lo + py)

    def z_peer(i):
        pz = lax.rem(z + i, 4)
        return (4 * x + 2 * (pz // 2) + core, 4 * lax.rem(pz, 2) + y)

    neighbours = [
        (far_gx, gy), (sib_gx, gy), (gx, low_gy), (gx, high_gy),
        (far_gx, low_gy), (far_gx, high_gy), (sib_gx, low_gy), (sib_gx, high_gy),
    ]
    peers = neighbours + [plane_peer(i)[1] for i in range(1, 16)] + [z_peer(i) for i in range(1, 4)]

    vol_copy = pltpu.make_async_copy(vol_ref, volb, l_sem.at[4])
    vol_copy.start()
    ker_copy = pltpu.make_async_copy(ker_hbm, ker_ref, l_sem.at[5])
    ker_copy.start()
    blocks = [(1, 0), (0, 1), (other, other), (core, core)]
    cot_copies = []
    for k, (p, m) in enumerate(blocks):
        copy = pltpu.make_async_copy(
            cot_ref.at[pl.ds(4 * p, 4), :, m], cotb.at[k], l_sem.at[k]
        )
        copy.start()
        cot_copies.append(copy)

    barrier = pltpu.get_barrier_semaphore()
    for peer in peers:
        pl.semaphore_signal(barrier, inc=1, device_id=peer, device_id_type=MESH)

    def turn_in(get, slot):
        turn[...] = get().astype(F32).reshape(64 * ROWS, 128)

        def row(n, _):
            vt[slot, :, lanes((n + 1) * 128, 128)] = turn[pl.ds(n, 64, stride=ROWS), :].astype(BF)
            return 0

        lax.fori_loop(0, ROWS, row, 0, unroll=True)

    vol_copy.wait()
    turn_in(lambda: volb[:, 0], 1)
    turn_in(lambda: volb[:, 1], 2)
    pl.semaphore_wait(barrier, len(peers))

    sends = [
        remote(volb.at[:, core], face.at[0], fs.at[0], fr.at[0], neighbours[0]),
        remote(volb.at[:, other], face.at[1], fs.at[1], fr.at[1], neighbours[1]),
    ]
    for copy in sends:
        copy.start()

    first, last = pl.ds(128, 128), pl.ds(ROWS * 128, 128)
    low, high = pl.ds(0, 128), pl.ds((ROWS + 1) * 128, 128)
    own = pl.ds(1, 2)
    ysends = [
        remote(vt.at[own, :, first], vt.at[own, :, high], fs.at[2], fr.at[2], neighbours[2]),
        remote(vt.at[own, :, last], vt.at[own, :, low], fs.at[3], fr.at[3], neighbours[3]),
    ]
    for k, (m, slot) in enumerate(((core, 3 - 3 * core), (other, 3 * core))):
        base = 4 + 2 * k
        ysends.append(remote(vt.at[1 + m, :, first], vt.at[slot, :, high], fs.at[base], fr.at[base], neighbours[base]))
        ysends.append(remote(vt.at[1 + m, :, last], vt.at[slot, :, low], fs.at[base + 1], fr.at[base + 1], neighbours[base + 1]))
    for copy in ysends:
        copy.start()
    sends += ysends

    half = jnp.asarray(0.5, BF)
    ker_copy.wait()
    for p in range(2):
        for q in range(2):
            pieces = [
                ker_ref[a, b].reshape(128, 64)
                for a in (1 + p, 3 - 3 * p)
                for b in (1 + q, 3 - 3 * q)
            ]
            ak[p, q] = jnp.concatenate(pieces, axis=1) * half
    for a in range(4):
        bk[a] = ker_ref[a].reshape(512, 64).astype(F32).T.astype(BF) * half
    g_s[:, :, :, :, 0:256] = jnp.zeros((2, 2, 2, 128, 256), BF)
    g_s[:, :, :, :, 256 + WIDE:] = jnp.zeros((2, 2, 2, 128, 256), BF)


    lane = lax.broadcasted_iota(jnp.int32, (32, 128), 1)

    def up(u):
        return jnp.where(lane == 0, 0.0, pltpu.roll(u, 1, axis=1))

    def down(u):
        return jnp.where(lane == 127, 0.0, pltpu.roll(u, 127, axis=1))

    def stacked(near, far, q, start, size):
        shift = 2 * q
        return jnp.concatenate(
            [
                vt[near, :, lanes(start + 128, size)],
                vt[near, :, lanes(start + 128 * shift, size)],
                vt[far, :, lanes(start + 128, size)],
                vt[far, :, lanes(start + 128 * shift, size)],
            ],
            axis=0,
        )

    def block(k):
        p, m = blocks[k]
        near, far = m + 1, m + 2 * p
        cot_copies[k].wait()
        cotf[...] = cotb[k].astype(F32).reshape(4 * 32 * ROWS, 128)

        def product(t, dst):
            q, ci = t // 4, lax.rem(t, 4)
            dst[...] = jnp.dot(
                ak[p, q], stacked(near, far, q, ci * 512, 512), preferred_element_type=F32
            )

        def finish(t, src):
            q, ci = t // 4, lax.rem(t, 4)
            for j in range(4):
                n = ci * 4 + j
                taps = [src[32 * c:32 * c + 32, 128 * j:128 * j + 128] for c in range(4)]
                halves = (taps[1] + up(taps[3]), taps[2] + down(taps[0]))
                grads = []
                for s in range(2):
                    rows = pl.ds((2 * q + s) * 32 * ROWS + n, 32, stride=ROWS)
                    t_h = jnp.tanh(halves[s])
                    w = 1.0 + t_h
                    act = halves[s] * w
                    actf[rows, :] = act
                    grads.append(cotf[rows, :] * (w + act * (1.0 - t_h)))
                four = (up(grads[1]), grads[0], grads[1], down(grads[0]))
                g_s[p, q, m, :, lanes((n + 2) * 128, 128)] = jnp.concatenate(
                    [value.astype(BF) for value in four], axis=0
                )

        product(0, ua)

        def pair(i, _):
            product(2 * i + 1, ub)
            finish(2 * i, ua)
            product(jnp.minimum(2 * i + 2, 7), ua)
            finish(2 * i + 1, ub)
            return 0

        lax.fori_loop(0, 4, pair, 0)
        for q in range(2):
            grad = nt_dot(g_s[p, q, m, :, 256:256 + WIDE], stacked(near, far, q, 0, WIDE))
            w_s[p, q] = grad if k < 2 else w_s[p, q] + grad
        act_ref[pl.ds(4 * p, 4), :, m] = actf[...].reshape(4, 32, ROWS, 128).astype(BF)

    ysends[0].wait_recv()
    ysends[1].wait_recv()

    @pl.when(first_y)
    def _():
        vt[own, :, low] = jnp.zeros((2, 64, 128), BF)

    @pl.when(last_y)
    def _():
        vt[own, :, high] = jnp.zeros((2, 64, 128), BF)

    block(0)
    block(1)

    def halo(index, slot):
        sends[index].wait_recv()
        turn_in(lambda: face[index], slot)
        sends[4 + 2 * index].wait_recv()
        sends[5 + 2 * index].wait_recv()

        @pl.when(first_y)
        def _():
            vt[slot, :, low] = jnp.zeros((64, 128), BF)

        @pl.when(last_y)
        def _():
            vt[slot, :, high] = jnp.zeros((64, 128), BF)

    halo(1, 3 - 3 * core)
    block(2)
    w_send[...] = w_s[other].reshape(256, 256).astype(BF)
    swap = remote(w_send, w_recv, ws.at[0], wr.at[0], neighbours[1])
    swap.start()

    halo(0, 3 * core)

    @pl.when(no_far)
    def _():
        vt[3 * core] = jnp.zeros((64, HALO), BF)

    block(3)

    swap.wait_recv()
    w_s[core] = w_s[core] + w_recv[...].astype(F32).reshape(2, 128, 256)
    w_bf[...] = w_s[core].reshape(256, 256).astype(BF)
    scatter = []
    for i in range(1, 16):
        index, peer = plane_peer(i)
        scatter.append(remote(w_bf.at[pl.ds(pl.multiple_of(16 * index, 16), 16)], rs_in.at[i], ws.at[1], wr.at[1], peer))
    for copy in scatter:
        copy.start()

    def back(target, terms, ci):
        total = None
        for a, p, m in terms:
            parts = [
                g_s[p, BACK[b][0], m, :, lanes((ci * 6 + 1 + BACK[b][1]) * 128, 768)]
                for b in range(4)
            ]
            product = jnp.dot(bk[a], jnp.concatenate(parts, axis=0), preferred_element_type=F32)
            total = product if total is None else total + product
        return total

    def outer(ci, _):
        igb[0, :, lanes(ci * 768, 768)] = back(0, ((3, 0, 0),), ci).astype(BF)
        igb[1, :, lanes(ci * 768, 768)] = back(3, ((0, 1, 1),), ci).astype(BF)
        return 0

    lax.fori_loop(0, 3, outer, 0)
    body = pl.ds(128, WIDE)
    bsends = [
        remote(igb.at[core, :, body], rx.at[0], bs.at[0], br.at[0], neighbours[0]),
        remote(igb.at[other, :, body], rx.at[1], bs.at[1], br.at[1], neighbours[1]),
    ]
    for copy in bsends:
        copy.start()

    def inner(ci, _):
        igf[0, :, lanes(ci * 768, 768)] = back(1, ((1, 0, 0), (2, 1, 0), (3, 0, 1)), ci)
        igf[1, :, lanes(ci * 768, 768)] = back(2, ((1, 0, 1), (2, 1, 1), (0, 1, 0)), ci)
        return 0

    lax.fori_loop(0, 3, inner, 0)
    igy[0] = igf[:, :, 0:128].astype(BF)
    igy[1] = igf[:, :, HALO - 128:].astype(BF)
    for k in range(2):
        bsends.append(remote(igy.at[k], ry.at[k], bs.at[2 + k], br.at[2 + k], neighbours[2 + k]))
    for index, m in ((0, core), (1, other)):
        for k, part_lanes in enumerate((low, high)):
            at = 4 + 2 * index + k
            bsends.append(remote(igb.at[m, :, part_lanes], rc.at[index, k], bs.at[at], br.at[at], neighbours[at]))
    for copy in bsends[2:]:
        copy.start()

    mine = 4 * x + y
    remote(w_bf.at[pl.ds(0, 240)].reshape(15, 16, 256), rs_in.at[pl.ds(1, 15)], ws.at[1], wr.at[1], neighbours[1]).wait_recv()
    q = mine // 8
    total = w_s[core, q, pl.ds(pl.multiple_of(16 * lax.rem(mine, 8), 16), 16)]
    for i in range(1, 16):
        total = total + rs_in[i].astype(F32)
    part[...] = total
    z_in[z] = total
    gather_z = [remote(part, z_in.at[z], ws.at[2], wr.at[2], z_peer(i)) for i in range(1, 4)]
    for copy in gather_z:
        copy.start()
    three = z_in.at[pl.ds(0, 3)]
    remote(three, three, ws.at[2], wr.at[2], neighbours[1]).wait_recv()
    total = (z_in[0] + z_in[1]) + (z_in[2] + z_in[3])
    fin[core, pl.ds(pl.multiple_of(16 * mine, 16), 16)] = (total * (0.5 * scaling)).astype(BF)
    spread = []
    for i in range(1, 16):
        _, peer = plane_peer(i)
        shard = fin.at[core, pl.ds(pl.multiple_of(16 * mine, 16), 16)]
        spread.append(remote(shard, shard, ws.at[3], wr.at[3], peer))
    for copy in spread:
        copy.start()

    def add(index, k, src, m, keep):
        place = (128, ROWS * 128)[k]

        @pl.when(keep)
        def _():
            igf[m, :, pl.ds(place, 128)] = igf[m, :, pl.ds(place, 128)] + src().astype(F32)

    bsends[2].wait_recv()
    bsends[3].wait_recv()
    for m in range(2):
        add(2, 1, lambda m=m: ry[0, m], m, jnp.logical_not(last_y))
        add(3, 0, lambda m=m: ry[1, m], m, jnp.logical_not(first_y))
    for index, m in ((1, other), (0, core)):
        ok = jnp.logical_not(no_far) if index == 0 else True
        bsends[index].wait_recv()
        bsends[4 + 2 * index].wait_recv()
        bsends[5 + 2 * index].wait_recv()

        def add_face(index=index, m=m):
            igf[m, :, body] = igf[m, :, body] + rx[index].astype(F32)

        if index == 0:
            pl.when(ok)(add_face)
        else:
            add_face()
        add(4, 1, lambda index=index: rc[index, 0], m, jnp.logical_and(ok, jnp.logical_not(last_y)))
        add(5, 0, lambda index=index: rc[index, 1], m, jnp.logical_and(ok, jnp.logical_not(first_y)))
        for n in range(ROWS):
            turn[pl.ds(n, 64, stride=ROWS), :] = igf[m, :, pl.ds((n + 1) * 128, 128)]
        igo[:, m] = turn[...].reshape(64, ROWS, 128).astype(BF)

    remote(w_bf.at[pl.ds(0, 240)], fin.at[core, pl.ds(0, 240)], ws.at[3], wr.at[3], neighbours[1]).wait_recv()
    both = remote(fin.at[core], fin.at[core], ws.at[4], wr.at[4], neighbours[1])
    both.start()
    both.wait_recv()
    for copy in sends + bsends + [swap, both]:
        copy.wait_send()
    remote(three, three, ws.at[2], wr.at[2], neighbours[1]).wait_send()
    remote(w_bf.at[pl.ds(0, 240)], fin.at[core, pl.ds(0, 240)], ws.at[1], wr.at[1], neighbours[1]).wait_send()
    remote(w_bf.at[pl.ds(0, 240)], fin.at[core, pl.ds(0, 240)], ws.at[3], wr.at[3], neighbours[1]).wait_send()


def write_kernel(act, ig, fin, act_ref, ig_ref, wg_ref, wgo, sem):
    copies = [
        pltpu.make_async_copy(act.at[pl.ds(2 * i, 2)], act_ref.at[pl.ds(2 * i, 2)], sem.at[i])
        for i in range(4)
    ]
    copies.append(pltpu.make_async_copy(ig, ig_ref, sem.at[4]))
    for copy in copies:
        copy.start()
    for p in range(2):
        for q in range(2):
            taps = [(a, b) for a in (1 + p, 3 - 3 * p) for b in (1 + q, 3 - 3 * q)]
            for i, (a, b) in enumerate(taps):
                value = fin[p, 128 * q:128 * q + 128, 64 * i:64 * i + 64]
                wgo[a, b] = value.astype(F32).reshape(4, 32, 64)
    copies.append(pltpu.make_async_copy(wgo, wg_ref, sem.at[5]))
    copies[-1].start()
    for copy in copies:
        copy.wait()


def on_device(volume, kernel, cotangent):
    cells = volume.shape[1] * volume.shape[2] * volume.shape[3]
    scaling = 1.0 / math.sqrt(cells * lax.axis_size("gx") * lax.axis_size("gy"))
    anywhere = pl.BlockSpec(memory_space=pltpu.HBM)
    inside = pl.BlockSpec(memory_space=pltpu.VMEM)
    dma = pltpu.SemaphoreType.DMA
    operands = [
        pltpu.with_memory_space_constraint(value, pltpu.HBM)
        for value in (volume, kernel, cotangent.reshape(8, 32, 2, ROWS, 128))
    ]
    results = pl.pallas_call(
        functools.partial(step_kernel, scaling),
        out_shape=(
            pltpu.VMEM((8, 32, 2, ROWS, 128), BF),
            pltpu.VMEM((64, 2, ROWS, 128), BF),
            pltpu.VMEM((2, 256, 256), BF),
        ),
        in_specs=[anywhere, anywhere, anywhere],
        out_specs=(inside, inside, inside),
        scratch_shapes=[
            pltpu.VMEM((64, 2, ROWS, 128), BF),
            pltpu.VMEM((4, 4, 4, 32, 64), BF),
            pltpu.VMEM((2, 64, ROWS, 128), BF),
            pltpu.VMEM((64 * ROWS, 128), F32),
            pltpu.VMEM((4, 64, HALO), BF),
            pltpu.VMEM((4, 4, 32, ROWS, 128), BF),
            pltpu.VMEM((4 * 32 * ROWS, 128), F32),
            pltpu.VMEM((4 * 32 * ROWS, 128), F32),
            pltpu.VMEM((128, 512), F32),
            pltpu.VMEM((128, 512), F32),
            pltpu.VMEM((2, 2, 2, 128, (ROWS + 4) * 128), BF),
            pltpu.VMEM((2, 2, 128, 256), BF),
            pltpu.VMEM((4, 64, 512), BF),
            pltpu.VMEM((2, 2, 128, 256), F32),
            pltpu.VMEM((256, 256), BF),
            pltpu.VMEM((256, 256), BF),
            pltpu.VMEM((256, 256), BF),
            pltpu.VMEM((16, 16, 256), BF),
            pltpu.VMEM((16, 256), F32),
            pltpu.VMEM((4, 16, 256), F32),
            pltpu.VMEM((2, 64, HALO), F32),
            pltpu.VMEM((2, 64, HALO), BF),
            pltpu.VMEM((2, 2, 64, 128), BF),
            pltpu.VMEM((2, 64, WIDE), BF),
            pltpu.VMEM((2, 2, 64, 128), BF),
            pltpu.VMEM((2, 2, 64, 128), BF),
            dma((6,)), dma((8,)), dma((8,)), dma((8,)), dma((8,)), dma((5,)), dma((5,)),
        ],
        compiler_params=pltpu.CompilerParams(
            collective_id=0, has_side_effects=True, vmem_limit_bytes=40 * 1024 * 1024
        ),
        name="conv_step",
    )(*operands)
    results = [pltpu.with_memory_space_constraint(value, pltpu.VMEM) for value in results]
    act, ig, wg = pl.pallas_call(
        write_kernel,
        out_shape=(
            jax.ShapeDtypeStruct((8, 32, 2, ROWS, 128), BF),
            jax.ShapeDtypeStruct((64, 2, ROWS, 128), BF),
            jax.ShapeDtypeStruct((4, 4, 4, 32, 64), F32),
        ),
        in_specs=[inside] * 3,
        out_specs=(anywhere,) * 3,
        scratch_shapes=[pltpu.VMEM((4, 4, 4, 32, 64), F32), dma((6,))],
        compiler_params=pltpu.CompilerParams(vmem_limit_bytes=16 * 1024 * 1024),
        name="write_out",
    )(*results)
    return act.reshape(2, 2, 2, 32, 2, ROWS, 128), ig, wg


def solution(mesh):
    placed = (P(None, "gx", "gy", None), P(), P(None, None, None, None, "gx", "gy", None))
    return jax.shard_map(
        on_device,
        mesh=mesh,
        in_specs=placed,
        out_specs=(P(None, None, None, None, "gx", "gy", None), P(None, "gx", "gy", None), P()),
        check_vma=False,
    )
```

```python
import functools
import math

import jax
import jax.numpy as jnp
from jax import lax
from jax.experimental import pallas as pl
from jax.experimental.pallas import tpu as pltpu
from jax.sharding import PartitionSpec as P

BF = jnp.bfloat16
F32 = jnp.float32
MESH = pl.DeviceIdType.MESH
BACK = ((1, -1), (0, 0), (1, 0), (0, 1))
ROWS = 16
WIDE = ROWS * 128
HALO = (ROWS + 2) * 128


def remote(src, dst, send, recv, device):
    return pltpu.make_async_remote_copy(
        src_ref=src, dst_ref=dst, send_sem=send, recv_sem=recv,
        device_id=device, device_id_type=MESH,
    )


def nt_dot(a, b):
    return lax.dot_general(a, b, (((1,), (1,)), ((), ())), preferred_element_type=F32)


def lanes(start, size):
    return pl.ds(pl.multiple_of(start, 128), size)


def step_kernel(
    scaling, vol_ref, ker_hbm, cot_ref, act_ref, igo, fin,
    volb, ker_ref, face, swap_rows, vt, cotb, cotn, actn, ua, ub, g_s, ak, bk, w_s,
    w_send, w_recv, w_bf, rs_in, part, z_in,
    igf, igb, igy, rx, ry, rc,
    l_sem, fs, fr, bs, br, ws, wr,
):
    gx, gy = lax.axis_index("gx"), lax.axis_index("gy")
    core = lax.rem(gx, 2)
    x, z_hi = gx // 4, lax.rem(gx // 2, 2)
    z_lo, y = gy // 4, lax.rem(gy, 4)
    z = 2 * z_hi + z_lo
    other = 1 - core
    far_gx = lax.rem(gx + 15 + 2 * core, 16)
    sib_gx = gx + 1 - 2 * core
    low_gy, high_gy = lax.rem(gy + 7, 8), lax.rem(gy + 1, 8)
    first_y, last_y = gy == 0, gy == 7
    no_far = jnp.logical_or(gx == 0, gx == 15)

    def plane_peer(i):
        px, py = lax.rem(x + i // 4, 4), lax.rem(y + i % 4, 4)
        return px * 4 + py, (px * 4 + 2 * z_hi + core, 4 * z_lo + py)

    def z_peer(i):
        pz = lax.rem(z + i, 4)
        return (4 * x + 2 * (pz // 2) + core, 4 * lax.rem(pz, 2) + y)

    neighbours = [
        (far_gx, gy), (sib_gx, gy), (gx, low_gy), (gx, high_gy),
        (far_gx, low_gy), (far_gx, high_gy), (sib_gx, low_gy), (sib_gx, high_gy),
    ]
    order = sorted(range(1, 16), key=lambda i: -(min(i // 4, 4 - i // 4) + min(i % 4, 4 - i % 4)))

    def twin(device):
        return (device[0] + 1 - 2 * core, device[1])

    plane = [plane_peer(i) for i in order]
    peers = neighbours + [d for _, d in plane] + [twin(d) for _, d in plane] + [z_peer(i) for i in range(1, 4)]

    vol_copy = pltpu.make_async_copy(vol_ref, volb, l_sem.at[4])
    vol_copy.start()
    ker_copy = pltpu.make_async_copy(ker_hbm, ker_ref, l_sem.at[5])
    ker_copy.start()
    blocks = [(1, 0), (0, 1), (other, other), (core, core)]
    cot_copies = []
    for k, (p, m) in enumerate(blocks):
        copy = pltpu.make_async_copy(
            cot_ref.at[pl.ds(4 * p, 4), :, m], cotb.at[k], l_sem.at[k]
        )
        copy.start()
        cot_copies.append(copy)

    barrier = pltpu.get_barrier_semaphore()
    for peer in peers:
        pl.semaphore_signal(barrier, inc=1, device_id=peer, device_id_type=MESH)

    down_i = lax.broadcasted_iota(jnp.int32, (256, 256), 0)
    along = lax.broadcasted_iota(jnp.int32, (256, 256), 1)
    swapped = jnp.bitwise_or(jnp.left_shift(jnp.bitwise_and(along, 15), 4), jnp.right_shift(along, 4))
    swap_rows[...] = jnp.where(down_i == swapped, 1.0, 0.0).astype(BF)

    def swap16(value):
        return jnp.dot(swap_rows[...], value, preferred_element_type=F32)

    def turn_in(left, right, put_left, put_right):
        both = swap16(jnp.concatenate([left.reshape(256, 128), right.reshape(256, 128)], axis=1)).astype(BF)
        for n in range(ROWS):
            put_left(n, both[16 * n:16 * n + 16, 0:128])
            put_right(n, both[16 * n:16 * n + 16, 128:256])

    def into(slot, group):
        def put(n, value):
            vt[slot, 16 * group:16 * group + 16, 128 * (n + 1):128 * (n + 2)] = value

        return put

    vol_copy.wait()
    for group in range(4):
        rows16 = slice(16 * group, 16 * group + 16)
        turn_in(volb[rows16, 0], volb[rows16, 1], into(1, group), into(2, group))
    pl.semaphore_wait(barrier, len(peers))

    sends = [
        remote(volb.at[:, core], face.at[0], fs.at[0], fr.at[0], neighbours[0]),
        remote(volb.at[:, other], face.at[1], fs.at[1], fr.at[1], neighbours[1]),
    ]
    first, last = pl.ds(128, 128), pl.ds(ROWS * 128, 128)
    low, high = pl.ds(0, 128), pl.ds((ROWS + 1) * 128, 128)
    own = pl.ds(1, 2)
    ysends = [
        remote(vt.at[own, :, first], vt.at[own, :, high], fs.at[2], fr.at[2], neighbours[2]),
        remote(vt.at[own, :, last], vt.at[own, :, low], fs.at[3], fr.at[3], neighbours[3]),
    ]
    for k, (m, slot) in enumerate(((core, 3 - 3 * core), (other, 3 * core))):
        base = 4 + 2 * k
        ysends.append(remote(vt.at[1 + m, :, first], vt.at[slot, :, high], fs.at[base], fr.at[base], neighbours[base]))
        ysends.append(remote(vt.at[1 + m, :, last], vt.at[slot, :, low], fs.at[base + 1], fr.at[base + 1], neighbours[base + 1]))
    for copy in ysends[:2] + sends + ysends[2:]:
        copy.start()
    sends += ysends

    half = jnp.asarray(0.5, BF)
    ker_copy.wait()
    for p in range(2):
        for q in range(2):
            pieces = [
                ker_ref[a, b].reshape(128, 64)
                for a in (1 + p, 3 - 3 * p)
                for b in (1 + q, 3 - 3 * q)
            ]
            ak[p, q] = jnp.concatenate(pieces, axis=1) * half
    for a in range(4):
        bk[a] = ker_ref[a].reshape(512, 64).astype(F32).T.astype(BF) * half
    w_s[...] = jnp.zeros((2, 2, 128, 256), F32)
    g_s[:, :, :, :, 0:256] = jnp.zeros((2, 2, 2, 128, 256), BF)
    g_s[:, :, :, :, 256 + WIDE:] = jnp.zeros((2, 2, 2, 128, 256), BF)


    lane = lax.broadcasted_iota(jnp.int32, (32, 128), 1)

    def up(u):
        return jnp.where(lane == 0, 0.0, pltpu.roll(u, 1, axis=1))

    def down(u):
        return jnp.where(lane == 127, 0.0, pltpu.roll(u, 127, axis=1))

    def stacked(near, far, q, start, size):
        shift = 2 * q
        return jnp.concatenate(
            [
                vt[near, :, lanes(start + 128, size)],
                vt[near, :, lanes(start + 128 * shift, size)],
                vt[far, :, lanes(start + 128, size)],
                vt[far, :, lanes(start + 128 * shift, size)],
            ],
            axis=0,
        )

    def block(k, p, m):
        near, far = m + 1, m + 2 * p

        def product(t):
            q, ci = t // 4, lax.rem(t, 4)
            return jnp.dot(
                ak[p, q], stacked(near, far, q, ci * 512, 512), preferred_element_type=F32
            )

        def finish(t, u):
            q, ci = t // 4, lax.rem(t, 4)
            for j in range(4):
                n = ci * 4 + j
                rows = pl.ds(pl.multiple_of(16 * n, 16), 16)
                taps = [u[32 * c:32 * c + 32, 128 * j:128 * j + 128] for c in range(4)]
                halves = (taps[1] + up(taps[3]), taps[2] + down(taps[0]))
                grads = []
                for s in range(2):
                    t_h = jnp.tanh(halves[s])
                    w = 1.0 + t_h
                    act = halves[s] * w
                    slope = w + act * (1.0 - t_h)
                    at = slice(128 * s, 128 * s + 128)
                    act = act.astype(BF)
                    for h in range(2):
                        actn[k, q, h, rows, at] = act[16 * h:16 * h + 16]
                    cot = jnp.concatenate([cotn[k, q, h, rows, at] for h in range(2)], axis=0)
                    grads.append(cot * slope)
                grads = [value.astype(BF) for value in grads]
                four = (
                    jnp.where(lane == 0, jnp.zeros((), BF), pltpu.roll(grads[1], 1, axis=1)),
                    grads[0],
                    grads[1],
                    jnp.where(lane == 127, jnp.zeros((), BF), pltpu.roll(grads[0], 127, axis=1)),
                )
                g_s[p, q, m, :, lanes((n + 2) * 128, 128)] = jnp.concatenate(four, axis=0)

        def grad(t):
            q, ci = t // 4, lax.rem(t, 4)
            w_s[p, q] += nt_dot(
                g_s[p, q, m, :, lanes((4 * ci + 2) * 128, 512)], stacked(near, far, q, ci * 512, 512)
            )

        ua[...] = product(0)
        ub[...] = product(1)
        finish(0, ua)

        def pair(i, _):
            t = 2 * i + 1
            grad(t - 1)
            ua[...] = product(t + 1)
            finish(t, ub)
            grad(t)
            ub[...] = product(t + 2)
            finish(t + 1, ua)
            return 0

        lax.fori_loop(0, 3, pair, 0)
        grad(6)
        finish(7, ub)
        grad(7)

    for copy in cot_copies:
        copy.wait()

    def turn_cot(i, _):
        k, q, h = i // 4, lax.rem(i // 2, 2), lax.rem(i, 2)
        pair = [
            cotb[k, 2 * q + s, pl.ds(16 * h, 16)].reshape(256, 128) for s in range(2)
        ]
        cotn[k, q, h] = swap16(jnp.concatenate(pair, axis=1))
        return 0

    lax.fori_loop(0, 16, turn_cot, 0)

    ysends[0].wait_recv()
    ysends[1].wait_recv()

    @pl.when(first_y)
    def _():
        vt[own, :, low] = jnp.zeros((2, 64, 128), BF)

    @pl.when(last_y)
    def _():
        vt[own, :, high] = jnp.zeros((2, 64, 128), BF)

    def early(k, _):
        block(k, 1 - k, k)
        return 0

    lax.fori_loop(0, 2, early, 0)

    def halo(index, slot):
        sends[index].wait_recv()
        for group in (0, 2):
            turn_in(
                face[index, 16 * group:16 * group + 16],
                face[index, 16 * group + 16:16 * group + 32],
                into(slot, group), into(slot, group + 1),
            )
        sends[4 + 2 * index].wait_recv()
        sends[5 + 2 * index].wait_recv()

        @pl.when(first_y)
        def _():
            vt[slot, :, low] = jnp.zeros((64, 128), BF)

        @pl.when(last_y)
        def _():
            vt[slot, :, high] = jnp.zeros((64, 128), BF)

    halo(1, 3 - 3 * core)
    block(2, other, other)
    w_send[...] = w_s[other].reshape(256, 256).astype(BF)
    swap = remote(w_send, w_recv, ws.at[0], wr.at[0], neighbours[1])
    swap.start()

    halo(0, 3 * core)

    @pl.when(no_far)
    def _():
        vt[3 * core] = jnp.zeros((64, HALO), BF)

    block(3, core, core)

    swap.wait_recv()
    w_s[core] = w_s[core] + w_recv[...].astype(F32).reshape(2, 128, 256)
    w_bf[...] = w_s[core].reshape(256, 256).astype(BF)
    scatter = []
    for i, (index, peer) in zip(order, plane):
        scatter.append(remote(w_bf.at[pl.ds(pl.multiple_of(16 * index, 16), 16)], rs_in.at[i], ws.at[1], wr.at[1], peer))
    for copy in scatter:
        copy.start()

    def back(target, terms, ci):
        total = None
        for a, p, m in terms:
            parts = [
                g_s[p, BACK[b][0], m, :, lanes((ci * 6 + 1 + BACK[b][1]) * 128, 768)]
                for b in range(4)
            ]
            product = jnp.dot(bk[a], jnp.concatenate(parts, axis=0), preferred_element_type=F32)
            total = product if total is None else total + product
        return total

    def outer(ci, _):
        igb[0, :, lanes(ci * 768, 768)] = back(0, ((3, 0, 0),), ci).astype(BF)
        igb[1, :, lanes(ci * 768, 768)] = back(3, ((0, 1, 1),), ci).astype(BF)
        return 0

    lax.fori_loop(0, 3, outer, 0)
    body = pl.ds(128, WIDE)
    bsends = [
        remote(igb.at[core, :, body], rx.at[0], bs.at[0], br.at[0], neighbours[0]),
        remote(igb.at[other, :, body], rx.at[1], bs.at[1], br.at[1], neighbours[1]),
    ]
    for copy in bsends:
        copy.start()

    def inner(ci, _):
        igf[0, :, lanes(ci * 768, 768)] = back(1, ((1, 0, 0), (2, 1, 0), (3, 0, 1)), ci)
        igf[1, :, lanes(ci * 768, 768)] = back(2, ((1, 0, 1), (2, 1, 1), (0, 1, 0)), ci)
        return 0

    lax.fori_loop(0, 3, inner, 0)
    igy[0] = igf[:, :, 0:128].astype(BF)
    igy[1] = igf[:, :, HALO - 128:].astype(BF)
    for k in range(2):
        bsends.append(remote(igy.at[k], ry.at[k], bs.at[2 + k], br.at[2 + k], neighbours[2 + k]))
    for index, m in ((0, core), (1, other)):
        for k, part_lanes in enumerate((low, high)):
            at = 4 + 2 * index + k
            bsends.append(remote(igb.at[m, :, part_lanes], rc.at[index, k], bs.at[at], br.at[at], neighbours[at]))
    for copy in bsends[2:]:
        copy.start()

    mine = 4 * x + y
    remote(w_bf.at[pl.ds(0, 240)].reshape(15, 16, 256), rs_in.at[pl.ds(1, 15)], ws.at[1], wr.at[1], neighbours[1]).wait_recv()
    q = mine // 8
    total = w_s[core, q, pl.ds(pl.multiple_of(16 * lax.rem(mine, 8), 16), 16)]
    for i in range(1, 16):
        total = total + rs_in[i].astype(F32)
    part[...] = total
    z_in[z] = total
    gather_z = [remote(part, z_in.at[z], ws.at[2], wr.at[2], z_peer(i)) for i in range(1, 4)]
    for copy in gather_z:
        copy.start()
    for k, (p, m) in enumerate(blocks):

        def turn_act(i, _, k=k, p=p, m=m):
            q, h = i // 2, lax.rem(i, 2)
            value = swap16(actn[k, q, h]).astype(BF)
            for s in range(2):
                act_ref[4 * p + 2 * q + s, pl.ds(16 * h, 16), m] = value[:, 128 * s:128 * s + 128].reshape(16, ROWS, 128)
            return 0

        lax.fori_loop(0, 4, turn_act, 0)

    three = z_in.at[pl.ds(0, 3)]
    remote(three, three, ws.at[2], wr.at[2], neighbours[1]).wait_recv()
    total = (z_in[0] + z_in[1]) + (z_in[2] + z_in[3])
    fin[core, pl.ds(pl.multiple_of(16 * mine, 16), 16)] = (total * (0.5 * scaling)).astype(BF)
    spread = []
    shard = fin.at[core, pl.ds(pl.multiple_of(16 * mine, 16), 16)]
    for _, peer in plane:
        spread.append(remote(shard, shard, ws.at[3], wr.at[3], peer))
        spread.append(remote(shard, shard, ws.at[4], wr.at[4], twin(peer)))
    spread.append(remote(shard, shard, ws.at[4], wr.at[4], neighbours[1]))
    for copy in spread:
        copy.start()

    def add(index, k, src, m, keep):
        place = (128, ROWS * 128)[k]

        @pl.when(keep)
        def _():
            igf[m, :, pl.ds(place, 128)] = igf[m, :, pl.ds(place, 128)] + src().astype(F32)

    bsends[2].wait_recv()
    bsends[3].wait_recv()
    for m in range(2):
        add(2, 1, lambda m=m: ry[0, m], m, jnp.logical_not(last_y))
        add(3, 0, lambda m=m: ry[1, m], m, jnp.logical_not(first_y))
    for index, m in ((1, other), (0, core)):
        ok = jnp.logical_not(no_far) if index == 0 else True
        bsends[index].wait_recv()
        bsends[4 + 2 * index].wait_recv()
        bsends[5 + 2 * index].wait_recv()

        def add_face(index=index, m=m):
            igf[m, :, body] = igf[m, :, body] + rx[index].astype(F32)

        if index == 0:
            pl.when(ok)(add_face)
        else:
            add_face()
        add(4, 1, lambda index=index: rc[index, 0], m, jnp.logical_and(ok, jnp.logical_not(last_y)))
        add(5, 0, lambda index=index: rc[index, 1], m, jnp.logical_and(ok, jnp.logical_not(first_y)))
        for group in (0, 2):
            halves = [
                jnp.concatenate(
                    [igf[m, 16 * g:16 * g + 16, 128 * (n + 1):128 * (n + 2)].astype(BF) for n in range(ROWS)], axis=0
                )
                for g in (group, group + 1)
            ]
            value = swap16(jnp.concatenate(halves, axis=1)).astype(BF)
            for g in range(2):
                at = 16 * (group + g)
                igo[at:at + 16, m] = value[:, 128 * g:128 * g + 128].reshape(16, ROWS, 128)
    remote(w_bf.at[pl.ds(0, 240)], fin.at[core, pl.ds(0, 240)], ws.at[3], wr.at[3], neighbours[1]).wait_recv()
    whole = remote(fin.at[core], fin.at[core], ws.at[4], wr.at[4], neighbours[1])
    whole.wait_recv()
    for copy in sends + bsends + [swap, whole]:
        copy.wait_send()
    remote(three, three, ws.at[2], wr.at[2], neighbours[1]).wait_send()
    remote(w_bf.at[pl.ds(0, 240)], fin.at[core, pl.ds(0, 240)], ws.at[1], wr.at[1], neighbours[1]).wait_send()
    remote(w_bf.at[pl.ds(0, 240)], fin.at[core, pl.ds(0, 240)], ws.at[3], wr.at[3], neighbours[1]).wait_send()


def write_kernel(act, ig, fin, act_ref, ig_ref, wg_ref, wgo, sem):
    copies = [
        pltpu.make_async_copy(act.at[pl.ds(2 * i, 2)], act_ref.at[pl.ds(2 * i, 2)], sem.at[i])
        for i in range(4)
    ]
    copies.append(pltpu.make_async_copy(ig, ig_ref, sem.at[4]))
    for copy in copies:
        copy.start()
    for p in range(2):
        for q in range(2):
            taps = [(a, b) for a in (1 + p, 3 - 3 * p) for b in (1 + q, 3 - 3 * q)]
            for i, (a, b) in enumerate(taps):
                value = fin[p, 128 * q:128 * q + 128, 64 * i:64 * i + 64]
                wgo[a, b] = value.astype(F32).reshape(4, 32, 64)
    copies.append(pltpu.make_async_copy(wgo, wg_ref, sem.at[5]))
    copies[-1].start()
    for copy in copies:
        copy.wait()


def on_device(volume, kernel, cotangent):
    cells = volume.shape[1] * volume.shape[2] * volume.shape[3]
    scaling = 1.0 / math.sqrt(cells * lax.axis_size("gx") * lax.axis_size("gy"))
    anywhere = pl.BlockSpec(memory_space=pltpu.HBM)
    inside = pl.BlockSpec(memory_space=pltpu.VMEM)
    dma = pltpu.SemaphoreType.DMA
    operands = [
        pltpu.with_memory_space_constraint(value, pltpu.HBM)
        for value in (volume, kernel, cotangent.reshape(8, 32, 2, ROWS, 128))
    ]
    results = pl.pallas_call(
        functools.partial(step_kernel, scaling),
        out_shape=(
            pltpu.VMEM((8, 32, 2, ROWS, 128), BF),
            pltpu.VMEM((64, 2, ROWS, 128), BF),
            pltpu.VMEM((2, 256, 256), BF),
        ),
        in_specs=[anywhere, anywhere, anywhere],
        out_specs=(inside, inside, inside),
        scratch_shapes=[
            pltpu.VMEM((64, 2, ROWS, 128), BF),
            pltpu.VMEM((4, 4, 4, 32, 64), BF),
            pltpu.VMEM((2, 64, ROWS, 128), BF),
            pltpu.VMEM((256, 256), BF),
            pltpu.VMEM((4, 64, HALO), BF),
            pltpu.VMEM((4, 4, 32, ROWS, 128), BF),
            pltpu.VMEM((4, 2, 2, 256, 256), F32),
            pltpu.VMEM((4, 2, 2, 256, 256), BF),
            pltpu.VMEM((128, 512), F32),
            pltpu.VMEM((128, 512), F32),
            pltpu.VMEM((2, 2, 2, 128, (ROWS + 4) * 128), BF),
            pltpu.VMEM((2, 2, 128, 256), BF),
            pltpu.VMEM((4, 64, 512), BF),
            pltpu.VMEM((2, 2, 128, 256), F32),
            pltpu.VMEM((256, 256), BF),
            pltpu.VMEM((256, 256), BF),
            pltpu.VMEM((256, 256), BF),
            pltpu.VMEM((16, 16, 256), BF),
            pltpu.VMEM((16, 256), F32),
            pltpu.VMEM((4, 16, 256), F32),
            pltpu.VMEM((2, 64, HALO), F32),
            pltpu.VMEM((2, 64, HALO), BF),
            pltpu.VMEM((2, 2, 64, 128), BF),
            pltpu.VMEM((2, 64, WIDE), BF),
            pltpu.VMEM((2, 2, 64, 128), BF),
            pltpu.VMEM((2, 2, 64, 128), BF),
            dma((6,)), dma((8,)), dma((8,)), dma((8,)), dma((8,)), dma((5,)), dma((5,)),
        ],
        compiler_params=pltpu.CompilerParams(
            collective_id=0, has_side_effects=True, vmem_limit_bytes=40 * 1024 * 1024
        ),
        name="conv_step",
    )(*operands)
    results = [pltpu.with_memory_space_constraint(value, pltpu.VMEM) for value in results]
    act, ig, wg = pl.pallas_call(
        write_kernel,
        out_shape=(
            jax.ShapeDtypeStruct((8, 32, 2, ROWS, 128), BF),
            jax.ShapeDtypeStruct((64, 2, ROWS, 128), BF),
            jax.ShapeDtypeStruct((4, 4, 4, 32, 64), F32),
        ),
        in_specs=[inside] * 3,
        out_specs=(anywhere,) * 3,
        scratch_shapes=[pltpu.VMEM((4, 4, 4, 32, 64), F32), dma((6,))],
        compiler_params=pltpu.CompilerParams(vmem_limit_bytes=16 * 1024 * 1024),
        name="write_out",
    )(*results)
    return act.reshape(2, 2, 2, 32, 2, ROWS, 128), ig, wg


def solution(mesh):
    placed = (P(None, "gx", "gy", None), P(), P(None, None, None, None, "gx", "gy", None))
    return jax.shard_map(
        on_device,
        mesh=mesh,
        in_specs=placed,
        out_specs=(P(None, None, None, None, "gx", "gy", None), P(None, "gx", "gy", None), P()),
        check_vma=False,
    )
```

```python
import functools
import math

import jax
import jax.numpy as jnp
from jax import lax
from jax.experimental import pallas as pl
from jax.experimental.pallas import tpu as pltpu
from jax.sharding import PartitionSpec as P

BF = jnp.bfloat16
F32 = jnp.float32
MESH = pl.DeviceIdType.MESH
BACK = ((1, -1), (0, 0), (1, 0), (0, 1))
ROWS = 16
WIDE = ROWS * 128
HALO = (ROWS + 2) * 128
EARLY = 2
LEAD = 8


def remote(src, dst, send, recv, device):
    return pltpu.make_async_remote_copy(
        src_ref=src, dst_ref=dst, send_sem=send, recv_sem=recv,
        device_id=device, device_id_type=MESH,
    )


def nt_dot(a, b):
    return lax.dot_general(a, b, (((1,), (1,)), ((), ())), preferred_element_type=F32)


def lanes(start, size):
    return pl.ds(pl.multiple_of(start, 128), size)


def step_kernel(
    scaling, vol_ref, ker_hbm, cot_ref, act_ref, igo, fin,
    volb, ker_ref, face, swap_rows, vt, cotb, cotn, actn, u_s, g_s, ak, bk, w_s,
    w_send, w_recv, w_bf, rs_in, part, z_in,
    igf, igb, igy, rx, ry, rc,
    l_sem, fs, fr, bs, br, ws, wr,
):
    gx, gy = lax.axis_index("gx"), lax.axis_index("gy")
    core = lax.rem(gx, 2)
    x, z_hi = gx // 4, lax.rem(gx // 2, 2)
    z_lo, y = gy // 4, lax.rem(gy, 4)
    z = 2 * z_hi + z_lo
    other = 1 - core
    far_gx = lax.rem(gx + 15 + 2 * core, 16)
    sib_gx = gx + 1 - 2 * core
    low_gy, high_gy = lax.rem(gy + 7, 8), lax.rem(gy + 1, 8)
    first_y, last_y = gy == 0, gy == 7
    no_far = jnp.logical_or(gx == 0, gx == 15)

    def plane_peer(i):
        px, py = lax.rem(x + i // 4, 4), lax.rem(y + i % 4, 4)
        return px * 4 + py, (px * 4 + 2 * z_hi + core, 4 * z_lo + py)

    def z_peer(i):
        pz = lax.rem(z + i, 4)
        return (4 * x + 2 * (pz // 2) + core, 4 * lax.rem(pz, 2) + y)

    neighbours = [
        (far_gx, gy), (sib_gx, gy), (gx, low_gy), (gx, high_gy),
        (far_gx, low_gy), (far_gx, high_gy), (sib_gx, low_gy), (sib_gx, high_gy),
    ]
    order = sorted(range(1, 16), key=lambda i: -(min(i // 4, 4 - i // 4) + min(i % 4, 4 - i % 4)))

    def twin(device):
        return (device[0] + 1 - 2 * core, device[1])

    plane = [plane_peer(i) for i in order]
    peers = neighbours + [d for _, d in plane] + [twin(d) for _, d in plane] + [z_peer(i) for i in range(1, 4)]

    vol_copy = pltpu.make_async_copy(vol_ref, volb, l_sem.at[4])
    vol_copy.start()
    ker_copy = pltpu.make_async_copy(ker_hbm, ker_ref, l_sem.at[5])
    ker_copy.start()
    blocks = [(1, 0), (0, 1), (other, other), (core, core)]
    cot_copies = []
    for k, (p, m) in enumerate(blocks):
        copy = pltpu.make_async_copy(
            cot_ref.at[pl.ds(4 * p, 4), :, m], cotb.at[k], l_sem.at[k]
        )
        copy.start()
        cot_copies.append(copy)

    barrier = pltpu.get_barrier_semaphore()
    for peer in peers:
        pl.semaphore_signal(barrier, inc=1, device_id=peer, device_id_type=MESH)

    down_i = lax.broadcasted_iota(jnp.int32, (256, 256), 0)
    along = lax.broadcasted_iota(jnp.int32, (256, 256), 1)
    swapped = jnp.bitwise_or(jnp.left_shift(jnp.bitwise_and(along, 15), 4), jnp.right_shift(along, 4))
    swap_rows[...] = jnp.where(down_i == swapped, 1.0, 0.0).astype(BF)

    def swap16(value):
        return jnp.dot(swap_rows[...], value, preferred_element_type=F32)

    def turn_in(left, right, put_left, put_right):
        both = swap16(jnp.concatenate([left.reshape(256, 128), right.reshape(256, 128)], axis=1)).astype(BF)
        for n in range(ROWS):
            put_left(n, both[16 * n:16 * n + 16, 0:128])
            put_right(n, both[16 * n:16 * n + 16, 128:256])

    def into(slot, group):
        def put(n, value):
            vt[slot, 16 * group:16 * group + 16, 128 * (n + 1):128 * (n + 2)] = value

        return put

    vol_copy.wait()
    for group in range(4):
        rows16 = slice(16 * group, 16 * group + 16)
        turn_in(volb[rows16, 0], volb[rows16, 1], into(1, group), into(2, group))
    pl.semaphore_wait(barrier, len(peers))

    sends = [
        remote(volb.at[:, core], face.at[0], fs.at[0], fr.at[0], neighbours[0]),
        remote(volb.at[:, other], face.at[1], fs.at[1], fr.at[1], neighbours[1]),
    ]
    first, last = pl.ds(128, 128), pl.ds(ROWS * 128, 128)
    low, high = pl.ds(0, 128), pl.ds((ROWS + 1) * 128, 128)
    own = pl.ds(1, 2)
    ysends = [
        remote(vt.at[own, :, first], vt.at[own, :, high], fs.at[2], fr.at[2], neighbours[2]),
        remote(vt.at[own, :, last], vt.at[own, :, low], fs.at[3], fr.at[3], neighbours[3]),
    ]
    for k, (m, slot) in enumerate(((core, 3 - 3 * core), (other, 3 * core))):
        base = 4 + 2 * k
        ysends.append(remote(vt.at[1 + m, :, first], vt.at[slot, :, high], fs.at[base], fr.at[base], neighbours[base]))
        ysends.append(remote(vt.at[1 + m, :, last], vt.at[slot, :, low], fs.at[base + 1], fr.at[base + 1], neighbours[base + 1]))
    for copy in ysends[:2] + sends + ysends[2:]:
        copy.start()
    sends += ysends

    half = jnp.asarray(0.5, BF)
    ker_copy.wait()
    for p in range(2):
        for q in range(2):
            pieces = [
                ker_ref[a, b].reshape(128, 64)
                for a in (3 - p, 1 - p)
                for b in (3 - q, 1 - q)
            ]
            ak[p, 128 * q:128 * q + 128] = jnp.concatenate(pieces, axis=1) * half
    for a in range(4):
        bk[a] = ker_ref[a].reshape(512, 64).astype(F32).T.astype(BF) * half
    w_s[...] = jnp.zeros((2, 256, 256), F32)
    vt[:, :, HALO:] = jnp.zeros((4, 64, 384), BF)
    for at, count in ((3, LEAD - 3), (LEAD + ROWS, 4)):
        g_s[:, :, :, :, 128 * at:128 * (at + count)] = jnp.zeros((2, 2, 2, 128, 128 * count), BF)

    lane = lax.broadcasted_iota(jnp.int32, (32, 128), 1)

    def up(u):
        return jnp.where(lane == 0, 0.0, pltpu.roll(u, 1, axis=1))

    def down(u):
        return jnp.where(lane == 127, 0.0, pltpu.roll(u, 127, axis=1))

    def group(members, weights, low_x, w_at):
        def tile(t):
            start = 512 * jnp.maximum(t, 0)
            return jnp.concatenate(
                [
                    vt[low_x + i, :, lanes(start + 128 * j, 512)]
                    for i in range(2)
                    for j in range(2)
                ],
                axis=0,
            )

        def product(t, slot):
            u = jnp.dot(weights(), tile(t), preferred_element_type=F32)
            u_s[slot, 0:len(members)] = u.reshape(len(members), 256, 512)

        def grad(t):
            rows = [
                g_s[p, q, m, :, lanes((4 * t - q + LEAD) * 128, 512)]
                for _, p, m in members
                for q in range(2)
            ]
            value = nt_dot(jnp.concatenate(rows, axis=0), tile(t))
            w_s[w_at] += value.reshape(len(members), 256, 256)

        def finish(t, slot, corners, sides):
            for member, (k, p, m) in enumerate(members):
                for j in range(corners):
                    for q in sides:
                        n = 4 * t + j - q
                        if j == 0 and q == 1:
                            outside = n < 0
                            put = jnp.where(outside, ROWS, n)
                            place = jnp.where(outside, LEAD + ROWS + 4, n + LEAD)
                            take = jnp.maximum(n, 0)
                        else:
                            put, place, take = n, n + LEAD, n
                        put = pl.ds(pl.multiple_of(16 * put, 16), 16)
                        take = pl.ds(pl.multiple_of(16 * take, 16), 16)
                        taps = [
                            u_s[slot, member, 128 * q + 32 * c:128 * q + 32 * c + 32, 128 * j:128 * j + 128]
                            for c in range(4)
                        ]
                        halves = (taps[1] + up(taps[3]), taps[2] + down(taps[0]))
                        grads = []
                        for s in range(2):
                            t_h = jnp.tanh(halves[s])
                            w = 1.0 + t_h
                            act = halves[s] * w
                            slope = w + act * (1.0 - t_h)
                            at = slice(128 * s, 128 * s + 128)
                            act = act.astype(BF)
                            for h in range(2):
                                actn[k, q, h, put, at] = act[16 * h:16 * h + 16]
                            cot = jnp.concatenate([cotn[k, q, h, take, at] for h in range(2)], axis=0)
                            grads.append((cot * slope).astype(BF))
                        four = (
                            jnp.where(lane == 0, jnp.zeros((), BF), pltpu.roll(grads[1], 1, axis=1)),
                            grads[0],
                            grads[1],
                            jnp.where(lane == 127, jnp.zeros((), BF), pltpu.roll(grads[0], 127, axis=1)),
                        )
                        g_s[p, q, m, :, lanes(place * 128, 128)] = jnp.concatenate(four, axis=0)

        product(0, 0)

        def step(t, _):
            now = lax.rem(t, 2)
            grad(t - 1)
            finish(t, now, 4, (0, 1))
            product(t + 1, 1 - now)
            return 0

        lax.fori_loop(0, ROWS // 4, step, 0)
        grad(ROWS // 4 - 1)
        finish(ROWS // 4, 0, 1, (1,))
        grad(ROWS // 4)

    for copy in cot_copies:
        copy.wait()

    def turn_cot(i, _):
        k, q, h = i // 4, lax.rem(i // 2, 2), lax.rem(i, 2)
        pair = [
            cotb[k, 2 * q + s, pl.ds(16 * h, 16)].reshape(256, 128) for s in range(2)
        ]
        cotn[k, q, h] = swap16(jnp.concatenate(pair, axis=1))
        return 0

    lax.fori_loop(0, 16, turn_cot, 0)

    ysends[0].wait_recv()
    ysends[1].wait_recv()

    @pl.when(first_y)
    def _():
        vt[own, :, low] = jnp.zeros((2, 64, 128), BF)

    @pl.when(last_y)
    def _():
        vt[own, :, high] = jnp.zeros((2, 64, 128), BF)

    group(
        [(1, 0, 1), (0, 1, 0)], lambda: ak[...].reshape(512, 256), 1, slice(0, 2)
    )

    def halo(index, slot):
        sends[index].wait_recv()
        for group in (0, 2):
            turn_in(
                face[index, 16 * group:16 * group + 16],
                face[index, 16 * group + 16:16 * group + 32],
                into(slot, group), into(slot, group + 1),
            )
        sends[4 + 2 * index].wait_recv()
        sends[5 + 2 * index].wait_recv()

        @pl.when(first_y)
        def _():
            vt[slot, :, low] = jnp.zeros((64, 128), BF)

        @pl.when(last_y)
        def _():
            vt[slot, :, high] = jnp.zeros((64, 128), BF)

    halo(1, 3 - 3 * core)
    group([(2, other, other)], lambda: ak[other], 2 * other, pl.ds(other, 1))
    w_send[...] = w_s[other].astype(BF)
    swap = remote(w_send, w_recv, ws.at[0], wr.at[0], neighbours[1])
    swap.start()

    halo(0, 3 * core)

    @pl.when(no_far)
    def _():
        vt[3 * core] = jnp.zeros((64, HALO + 384), BF)

    group([(3, core, core)], lambda: ak[core], 2 * core, pl.ds(core, 1))

    swap.wait_recv()
    w_s[core] = w_s[core] + w_recv[...].astype(F32)
    w_bf[...] = w_s[core].astype(BF)
    scatter = []
    for i, (index, peer) in zip(order, plane):
        scatter.append(remote(w_bf.at[pl.ds(pl.multiple_of(16 * index, 16), 16)], rs_in.at[i], ws.at[1], wr.at[1], peer))
    for copy in scatter:
        copy.start()

    def back(target, terms, ci):
        total = None
        for a, p, m in terms:
            parts = [
                g_s[p, BACK[b][0], m, :, lanes((ci * 6 + LEAD - 1 + BACK[b][1]) * 128, 768)]
                for b in range(4)
            ]
            product = jnp.dot(bk[a], jnp.concatenate(parts, axis=0), preferred_element_type=F32)
            total = product if total is None else total + product
        return total

    def outer(ci, _):
        igb[0, :, lanes(ci * 768, 768)] = back(0, ((3, 0, 0),), ci).astype(BF)
        igb[1, :, lanes(ci * 768, 768)] = back(3, ((0, 1, 1),), ci).astype(BF)
        return 0

    lax.fori_loop(0, 3, outer, 0)
    body = pl.ds(128, WIDE)
    far_parts = []
    for g in range(4):
        rows16, at = pl.ds(16 * g, 16), 0 if g == 0 else 7 + g
        far_parts.append(
            remote(igb.at[core, rows16, body], rx.at[0, rows16], bs.at[at], br.at[at], neighbours[0])
        )
    bsends = [
        far_parts[0],
        remote(igb.at[other, :, body], rx.at[1], bs.at[1], br.at[1], neighbours[1]),
    ]
    for copy in far_parts[:EARLY] + bsends[1:]:
        copy.start()

    def inner(ci, _):
        igf[0, :, lanes(ci * 768, 768)] = back(1, ((1, 0, 0), (2, 1, 0), (3, 0, 1)), ci)
        igf[1, :, lanes(ci * 768, 768)] = back(2, ((1, 0, 1), (2, 1, 1), (0, 1, 0)), ci)
        return 0

    lax.fori_loop(0, 3, inner, 0)
    igy[0] = igf[:, :, 0:128].astype(BF)
    igy[1] = igf[:, :, HALO - 128:].astype(BF)
    for k in range(2):
        bsends.append(remote(igy.at[k], ry.at[k], bs.at[2 + k], br.at[2 + k], neighbours[2 + k]))
    for index, m in ((0, core), (1, other)):
        for k, part_lanes in enumerate((low, high)):
            at = 4 + 2 * index + k
            bsends.append(remote(igb.at[m, :, part_lanes], rc.at[index, k], bs.at[at], br.at[at], neighbours[at]))
    for copy in bsends[2:]:
        copy.start()

    mine = 4 * x + y
    remote(w_bf.at[pl.ds(0, 240)].reshape(15, 16, 256), rs_in.at[pl.ds(1, 15)], ws.at[1], wr.at[1], neighbours[1]).wait_recv()
    total = w_s[core, pl.ds(pl.multiple_of(16 * mine, 16), 16)]
    for i in range(1, 16):
        total = total + rs_in[i].astype(F32)
    part[...] = total.astype(BF)
    z_in[z] = total.astype(BF)
    gather_z = [remote(part, z_in.at[z], ws.at[2], wr.at[2], z_peer(i)) for i in (2, 1, 3)]
    for copy in gather_z + far_parts[EARLY:3]:
        copy.start()
    for k, (p, m) in enumerate(blocks):

        def turn_act(i, _, k=k, p=p, m=m):
            q, h = i // 2, lax.rem(i, 2)
            value = swap16(actn[k, q, h, 0:256]).astype(BF)
            for s in range(2):
                act_ref[4 * p + 2 * q + s, pl.ds(16 * h, 16), m] = value[:, 128 * s:128 * s + 128].reshape(16, ROWS, 128)
            return 0

        lax.fori_loop(0, 4, turn_act, 0)

    three = z_in.at[pl.ds(0, 3)]
    remote(three, three, ws.at[2], wr.at[2], neighbours[1]).wait_recv()
    wide = [z_in[i].astype(F32) for i in range(4)]
    total = (wide[0] + wide[1]) + (wide[2] + wide[3])
    fin[core, pl.ds(pl.multiple_of(16 * mine, 16), 16)] = (total * (0.5 * scaling)).astype(BF)
    spread = []
    shard = fin.at[core, pl.ds(pl.multiple_of(16 * mine, 16), 16)]
    for _, peer in plane:
        spread.append(remote(shard, shard, ws.at[3], wr.at[3], peer))
        spread.append(remote(shard, shard, ws.at[4], wr.at[4], twin(peer)))
    spread.append(remote(shard, shard, ws.at[4], wr.at[4], neighbours[1]))
    for copy in spread + far_parts[3:]:
        copy.start()

    def add(index, k, src, m, keep):
        place = (128, ROWS * 128)[k]

        @pl.when(keep)
        def _():
            igf[m, :, pl.ds(place, 128)] = igf[m, :, pl.ds(place, 128)] + src().astype(F32)

    bsends[2].wait_recv()
    bsends[3].wait_recv()
    for m in range(2):
        add(2, 1, lambda m=m: ry[0, m], m, jnp.logical_not(last_y))
        add(3, 0, lambda m=m: ry[1, m], m, jnp.logical_not(first_y))
    for index, m in ((1, other), (0, core)):
        ok = jnp.logical_not(no_far) if index == 0 else True
        for copy in far_parts if index == 0 else [bsends[1]]:
            copy.wait_recv()
        bsends[4 + 2 * index].wait_recv()
        bsends[5 + 2 * index].wait_recv()

        def add_face(index=index, m=m):
            igf[m, :, body] = igf[m, :, body] + rx[index].astype(F32)

        if index == 0:
            pl.when(ok)(add_face)
        else:
            add_face()
        add(4, 1, lambda index=index: rc[index, 0], m, jnp.logical_and(ok, jnp.logical_not(last_y)))
        add(5, 0, lambda index=index: rc[index, 1], m, jnp.logical_and(ok, jnp.logical_not(first_y)))
        for group in (0, 2):
            halves = [
                jnp.concatenate(
                    [igf[m, 16 * g:16 * g + 16, 128 * (n + 1):128 * (n + 2)].astype(BF) for n in range(ROWS)], axis=0
                )
                for g in (group, group + 1)
            ]
            value = swap16(jnp.concatenate(halves, axis=1)).astype(BF)
            for g in range(2):
                at = 16 * (group + g)
                igo[at:at + 16, m] = value[:, 128 * g:128 * g + 128].reshape(16, ROWS, 128)
    remote(w_bf.at[pl.ds(0, 240)], fin.at[core, pl.ds(0, 240)], ws.at[3], wr.at[3], neighbours[1]).wait_recv()
    whole = remote(fin.at[core], fin.at[core], ws.at[4], wr.at[4], neighbours[1])
    whole.wait_recv()
    for copy in sends + bsends + far_parts[1:] + [swap, whole]:
        copy.wait_send()
    remote(three, three, ws.at[2], wr.at[2], neighbours[1]).wait_send()
    remote(w_bf.at[pl.ds(0, 240)], fin.at[core, pl.ds(0, 240)], ws.at[1], wr.at[1], neighbours[1]).wait_send()
    remote(w_bf.at[pl.ds(0, 240)], fin.at[core, pl.ds(0, 240)], ws.at[3], wr.at[3], neighbours[1]).wait_send()


def write_kernel(act, ig, fin, act_ref, ig_ref, wg_ref, wgo, sem):
    copies = [
        pltpu.make_async_copy(act.at[pl.ds(2 * i, 2)], act_ref.at[pl.ds(2 * i, 2)], sem.at[i])
        for i in range(4)
    ]
    copies.append(pltpu.make_async_copy(ig, ig_ref, sem.at[4]))
    for copy in copies:
        copy.start()
    for p in range(2):
        for q in range(2):
            taps = [(a, b) for a in (3 - p, 1 - p) for b in (3 - q, 1 - q)]
            for i, (a, b) in enumerate(taps):
                value = fin[p, 128 * q:128 * q + 128, 64 * i:64 * i + 64]
                wgo[a, b] = value.astype(F32).reshape(4, 32, 64)
    copies.append(pltpu.make_async_copy(wgo, wg_ref, sem.at[5]))
    copies[-1].start()
    for copy in copies:
        copy.wait()


def on_device(volume, kernel, cotangent):
    cells = volume.shape[1] * volume.shape[2] * volume.shape[3]
    scaling = 1.0 / math.sqrt(cells * lax.axis_size("gx") * lax.axis_size("gy"))
    anywhere = pl.BlockSpec(memory_space=pltpu.HBM)
    inside = pl.BlockSpec(memory_space=pltpu.VMEM)
    dma = pltpu.SemaphoreType.DMA
    operands = [
        pltpu.with_memory_space_constraint(value, pltpu.HBM)
        for value in (volume, kernel, cotangent.reshape(8, 32, 2, ROWS, 128))
    ]
    results = pl.pallas_call(
        functools.partial(step_kernel, scaling),
        out_shape=(
            pltpu.VMEM((8, 32, 2, ROWS, 128), BF),
            pltpu.VMEM((64, 2, ROWS, 128), BF),
            pltpu.VMEM((2, 256, 256), BF),
        ),
        in_specs=[anywhere, anywhere, anywhere],
        out_specs=(inside, inside, inside),
        scratch_shapes=[
            pltpu.VMEM((64, 2, ROWS, 128), BF),
            pltpu.VMEM((4, 4, 4, 32, 64), BF),
            pltpu.VMEM((2, 64, ROWS, 128), BF),
            pltpu.VMEM((256, 256), BF),
            pltpu.VMEM((4, 64, HALO + 384), BF),
            pltpu.VMEM((4, 4, 32, ROWS, 128), BF),
            pltpu.VMEM((4, 2, 2, 256, 256), F32),
            pltpu.VMEM((4, 2, 2, 16 + 256, 256), BF),
            pltpu.VMEM((2, 2, 256, 512), F32),
            pltpu.VMEM((2, 2, 2, 128, (LEAD + ROWS + 5) * 128), BF),
            pltpu.VMEM((2, 256, 256), BF),
            pltpu.VMEM((4, 64, 512), BF),
            pltpu.VMEM((2, 256, 256), F32),
            pltpu.VMEM((256, 256), BF),
            pltpu.VMEM((256, 256), BF),
            pltpu.VMEM((256, 256), BF),
            pltpu.VMEM((16, 16, 256), BF),
            pltpu.VMEM((16, 256), BF),
            pltpu.VMEM((4, 16, 256), BF),
            pltpu.VMEM((2, 64, HALO), F32),
            pltpu.VMEM((2, 64, HALO), BF),
            pltpu.VMEM((2, 2, 64, 128), BF),
            pltpu.VMEM((2, 64, WIDE), BF),
            pltpu.VMEM((2, 2, 64, 128), BF),
            pltpu.VMEM((2, 2, 64, 128), BF),
            dma((6,)), dma((8,)), dma((8,)), dma((11,)), dma((11,)), dma((5,)), dma((5,)),
        ],
        compiler_params=pltpu.CompilerParams(
            collective_id=0, has_side_effects=True, vmem_limit_bytes=40 * 1024 * 1024
        ),
        name="conv_step",
    )(*operands)
    results = [pltpu.with_memory_space_constraint(value, pltpu.VMEM) for value in results]
    act, ig, wg = pl.pallas_call(
        write_kernel,
        out_shape=(
            jax.ShapeDtypeStruct((8, 32, 2, ROWS, 128), BF),
            jax.ShapeDtypeStruct((64, 2, ROWS, 128), BF),
            jax.ShapeDtypeStruct((4, 4, 4, 32, 64), F32),
        ),
        in_specs=[inside] * 3,
        out_specs=(anywhere,) * 3,
        scratch_shapes=[pltpu.VMEM((4, 4, 4, 32, 64), F32), dma((6,))],
        compiler_params=pltpu.CompilerParams(vmem_limit_bytes=16 * 1024 * 1024),
        name="write_out",
    )(*results)
    return act.reshape(2, 2, 2, 32, 2, ROWS, 128), ig, wg


def solution(mesh):
    placed = (P(None, "gx", "gy", None), P(), P(None, None, None, None, "gx", "gy", None))
    return jax.shard_map(
        on_device,
        mesh=mesh,
        in_specs=placed,
        out_specs=(P(None, None, None, None, "gx", "gy", None), P(None, "gx", "gy", None), P()),
        check_vma=False,
    )
```

```python
import functools
import math

import jax
import jax.numpy as jnp
from jax import lax
from jax.experimental import pallas as pl
from jax.experimental.pallas import tpu as pltpu
from jax.sharding import PartitionSpec as P

BF = jnp.bfloat16
F32 = jnp.float32
MESH = pl.DeviceIdType.MESH
BACK = ((1, -1), (0, 0), (1, 0), (0, 1))
ROWS = 16
WIDE = ROWS * 128
HALO = (ROWS + 2) * 128
EARLY = 2
LEAD = 8


def remote(src, dst, send, recv, device):
    return pltpu.make_async_remote_copy(
        src_ref=src, dst_ref=dst, send_sem=send, recv_sem=recv,
        device_id=device, device_id_type=MESH,
    )


def nt_dot(a, b):
    return lax.dot_general(a, b, (((1,), (1,)), ((), ())), preferred_element_type=F32)


def lanes(start, size):
    return pl.ds(pl.multiple_of(start, 128), size)


def step_kernel(
    scaling, vol_ref, ker_hbm, cot_ref, act_ref, igo, fin,
    volb, ker_ref, face, swap_rows, vt, cotb, cotn, actn, u_s, g_s, ak, bk, w_s,
    w_send, w_recv, w_bf, rs_in, part, z_in,
    igf, igb, igy, rx, ry, rc,
    l_sem, fs, fr, bs, br, ws, wr,
):
    gx, gy = lax.axis_index("gx"), lax.axis_index("gy")
    core = lax.rem(gx, 2)
    x, z_hi = gx // 4, lax.rem(gx // 2, 2)
    z_lo, y = gy // 4, lax.rem(gy, 4)
    z = 2 * z_hi + z_lo
    other = 1 - core
    far_gx = lax.rem(gx + 15 + 2 * core, 16)
    sib_gx = gx + 1 - 2 * core
    low_gy, high_gy = lax.rem(gy + 7, 8), lax.rem(gy + 1, 8)
    first_y, last_y = gy == 0, gy == 7
    no_far = jnp.logical_or(gx == 0, gx == 15)

    def plane_peer(i):
        px, py = lax.rem(x + i // 4, 4), lax.rem(y + i % 4, 4)
        return px * 4 + py, (px * 4 + 2 * z_hi + core, 4 * z_lo + py)

    def z_peer(i):
        pz = lax.rem(z + i, 4)
        return (4 * x + 2 * (pz // 2) + core, 4 * lax.rem(pz, 2) + y)

    neighbours = [
        (far_gx, gy), (sib_gx, gy), (gx, low_gy), (gx, high_gy),
        (far_gx, low_gy), (far_gx, high_gy), (sib_gx, low_gy), (sib_gx, high_gy),
    ]
    order = sorted(range(1, 16), key=lambda i: -(min(i // 4, 4 - i // 4) + min(i % 4, 4 - i % 4)))

    def twin(device):
        return (device[0] + 1 - 2 * core, device[1])

    plane = [plane_peer(i) for i in order]
    peers = neighbours + [d for _, d in plane] + [twin(d) for _, d in plane] + [z_peer(i) for i in range(1, 4)]

    vol_copy = pltpu.make_async_copy(vol_ref, volb, l_sem.at[4])
    vol_copy.start()
    ker_copy = pltpu.make_async_copy(ker_hbm, ker_ref, l_sem.at[5])
    ker_copy.start()
    blocks = [(1, 0), (0, 1), (other, other), (core, core)]
    cot_copies = []
    for k, (p, m) in enumerate(blocks):
        copy = pltpu.make_async_copy(
            cot_ref.at[pl.ds(4 * p, 4), :, m], cotb.at[k], l_sem.at[k]
        )
        copy.start()
        cot_copies.append(copy)

    barrier = pltpu.get_barrier_semaphore()
    for peer in peers:
        pl.semaphore_signal(barrier, inc=1, device_id=peer, device_id_type=MESH)

    down_i = lax.broadcasted_iota(jnp.int32, (256, 256), 0)
    along = lax.broadcasted_iota(jnp.int32, (256, 256), 1)
    swapped = jnp.bitwise_or(jnp.left_shift(jnp.bitwise_and(along, 15), 4), jnp.right_shift(along, 4))
    swap_rows[...] = jnp.where(down_i == swapped, 1.0, 0.0).astype(BF)

    def swap16(value):
        return jnp.dot(swap_rows[...], value, preferred_element_type=F32)

    def turn_in(left, right, put_left, put_right):
        both = swap16(jnp.concatenate([left.reshape(256, 128), right.reshape(256, 128)], axis=1)).astype(BF)
        for n in range(ROWS):
            put_left(n, both[16 * n:16 * n + 16, 0:128])
            put_right(n, both[16 * n:16 * n + 16, 128:256])

    def into(slot, group):
        def put(n, value):
            vt[slot, 16 * group:16 * group + 16, 128 * (n + 1):128 * (n + 2)] = value

        return put

    vol_copy.wait()
    for group in range(4):
        rows16 = slice(16 * group, 16 * group + 16)
        turn_in(volb[rows16, 0], volb[rows16, 1], into(1, group), into(2, group))
    pl.semaphore_wait(barrier, len(peers))

    sends = [
        remote(volb.at[:, core], face.at[0], fs.at[0], fr.at[0], neighbours[0]),
        remote(volb.at[:, other], face.at[1], fs.at[1], fr.at[1], neighbours[1]),
    ]
    first, last = pl.ds(128, 128), pl.ds(ROWS * 128, 128)
    low, high = pl.ds(0, 128), pl.ds((ROWS + 1) * 128, 128)
    own = pl.ds(1, 2)
    ysends = [
        remote(vt.at[own, :, first], vt.at[own, :, high], fs.at[2], fr.at[2], neighbours[2]),
        remote(vt.at[own, :, last], vt.at[own, :, low], fs.at[3], fr.at[3], neighbours[3]),
    ]
    for k, (m, slot) in enumerate(((core, 3 - 3 * core), (other, 3 * core))):
        base = 4 + 2 * k
        ysends.append(remote(vt.at[1 + m, :, first], vt.at[slot, :, high], fs.at[base], fr.at[base], neighbours[base]))
        ysends.append(remote(vt.at[1 + m, :, last], vt.at[slot, :, low], fs.at[base + 1], fr.at[base + 1], neighbours[base + 1]))
    for copy in ysends[:2] + sends + ysends[2:]:
        copy.start()
    sends += ysends

    half = jnp.asarray(0.5, BF)
    ker_copy.wait()
    for p in range(2):
        for q in range(2):
            pieces = [
                ker_ref[a, b].reshape(128, 64)
                for a in (3 - p, 1 - p)
                for b in (3 - q, 1 - q)
            ]
            ak[p, 128 * q:128 * q + 128] = jnp.concatenate(pieces, axis=1) * half
    for a in range(4):
        bk[a] = ker_ref[a].reshape(512, 64).astype(F32).T.astype(BF) * half
    w_s[...] = jnp.zeros((2, 256, 256), F32)
    for at, count in ((LEAD - 4, 5), (LEAD + ROWS, 2)):
        g_s[:, :, :, :, 128 * at:128 * (at + count)] = jnp.zeros((2, 2, 2, 128, 128 * count), BF)

    lane = lax.broadcasted_iota(jnp.int32, (32, 128), 1)

    def up(u):
        return jnp.where(lane == 0, 0.0, pltpu.roll(u, 1, axis=1))

    def down(u):
        return jnp.where(lane == 127, 0.0, pltpu.roll(u, 127, axis=1))

    def group(members, weights, low_x, w_at, between=None):
        def tile(start, size):
            return jnp.concatenate(
                [
                    vt[low_x + i, :, lanes(start + 128 * j, size)]
                    for i in range(2)
                    for j in range(2)
                ],
                axis=0,
            )

        def product(t, slot):
            u = jnp.dot(weights(), tile(512 * t + 128, 512), preferred_element_type=F32)
            u_s[slot, 0:len(members)] = u.reshape(len(members), 256, 512)

        def grad(first, size):
            rows = [
                g_s[p, q, m, :, lanes((first - q + LEAD) * 128, size)]
                for _, p, m in members
                for q in range(2)
            ]
            value = nt_dot(jnp.concatenate(rows, axis=0), tile(128 * (jnp.maximum(first, 1) if size == 512 else first), size))
            w_s[w_at] += value.reshape(len(members), 256, 256)

        def finish(first, slot, corners, sides):
            for member, (k, p, m) in enumerate(members):
                for j in range(corners):
                    for q in sides:
                        n = first + j - q
                        if j == 3 and q == 0:
                            outside = n == ROWS
                            put = n
                            place = jnp.where(outside, LEAD + ROWS + 2, n + LEAD)
                            take = jnp.minimum(n, ROWS - 1)
                        else:
                            put, place, take = n, n + LEAD, n
                        put = pl.ds(pl.multiple_of(16 * put, 16), 16)
                        take = pl.ds(pl.multiple_of(16 * take, 16), 16)
                        taps = [
                            u_s[slot, member, 128 * q + 32 * c:128 * q + 32 * c + 32, 128 * j:128 * j + 128]
                            for c in range(4)
                        ]
                        halves = (taps[1] + up(taps[3]), taps[2] + down(taps[0]))
                        grads = []
                        for s in range(2):
                            t_h = jnp.tanh(halves[s])
                            w = 1.0 + t_h
                            act = halves[s] * w
                            slope = w + act * (1.0 - t_h)
                            at = slice(128 * s, 128 * s + 128)
                            act = act.astype(BF)
                            for h in range(2):
                                actn[k, q, h, put, at] = act[16 * h:16 * h + 16]
                            cot = jnp.concatenate([cotn[k, q, h, take, at] for h in range(2)], axis=0)
                            grads.append((cot * slope).astype(BF))
                        four = (
                            jnp.where(lane == 0, jnp.zeros((), BF), pltpu.roll(grads[1], 1, axis=1)),
                            grads[0],
                            grads[1],
                            jnp.where(lane == 127, jnp.zeros((), BF), pltpu.roll(grads[0], 127, axis=1)),
                        )
                        g_s[p, q, m, :, lanes(place * 128, 128)] = jnp.concatenate(four, axis=0)

        product(0, 0)

        def step(t, _):
            now = lax.rem(t, 2)
            grad(4 * t - 3, 512)
            finish(4 * t + 1, now, 4, (0, 1))
            product(jnp.minimum(t + 1, 3), 1 - now)
            return 0

        if between is None:
            lax.fori_loop(0, 4, step, 0)
        else:
            lax.fori_loop(0, 2, step, 0)
            between()
            lax.fori_loop(2, 4, step, 0)
        u = jnp.dot(weights(), tile(0, 128), preferred_element_type=F32)
        u_s[1, 0:len(members), :, 0:128] = u.reshape(len(members), 256, 128)
        grad(13, 512)
        finish(0, 1, 1, (0,))
        grad(0, 128)

    for copy in cot_copies:
        copy.wait()

    def turn_cot(i, _):
        k, q, h = i // 4, lax.rem(i // 2, 2), lax.rem(i, 2)
        pair = [
            cotb[k, 2 * q + s, pl.ds(16 * h, 16)].reshape(256, 128) for s in range(2)
        ]
        cotn[k, q, h] = swap16(jnp.concatenate(pair, axis=1))
        return 0

    lax.fori_loop(0, 16, turn_cot, 0)

    def y_rows():
        ysends[0].wait_recv()
        ysends[1].wait_recv()

        @pl.when(first_y)
        def _():
            vt[own, :, low] = jnp.zeros((2, 64, 128), BF)

        @pl.when(last_y)
        def _():
            vt[own, :, high] = jnp.zeros((2, 64, 128), BF)

    group(
        [(1, 0, 1), (0, 1, 0)], lambda: ak[...].reshape(512, 256), 1, slice(0, 2), y_rows
    )

    def halo(index, slot):
        sends[index].wait_recv()
        for group in (0, 2):
            turn_in(
                face[index, 16 * group:16 * group + 16],
                face[index, 16 * group + 16:16 * group + 32],
                into(slot, group), into(slot, group + 1),
            )
        sends[4 + 2 * index].wait_recv()
        sends[5 + 2 * index].wait_recv()

        @pl.when(first_y)
        def _():
            vt[slot, :, low] = jnp.zeros((64, 128), BF)

        @pl.when(last_y)
        def _():
            vt[slot, :, high] = jnp.zeros((64, 128), BF)

    halo(1, 3 - 3 * core)
    group([(2, other, other)], lambda: ak[other], 2 * other, pl.ds(other, 1))
    w_send[...] = w_s[other].astype(BF)
    swap = remote(w_send, w_recv, ws.at[0], wr.at[0], neighbours[1])
    swap.start()

    halo(0, 3 * core)

    @pl.when(no_far)
    def _():
        vt[3 * core] = jnp.zeros((64, HALO), BF)

    group([(3, core, core)], lambda: ak[core], 2 * core, pl.ds(core, 1))

    swap.wait_recv()
    w_s[core] = w_s[core] + w_recv[...].astype(F32)
    w_bf[...] = w_s[core].astype(BF)
    scatter = []
    for i, (index, peer) in zip(order, plane):
        scatter.append(remote(w_bf.at[pl.ds(pl.multiple_of(16 * index, 16), 16)], rs_in.at[i], ws.at[1], wr.at[1], peer))
    for copy in scatter:
        copy.start()

    def back(target, terms, ci):
        total = None
        for a, p, m in terms:
            parts = [
                g_s[p, BACK[b][0], m, :, lanes((ci * 6 + LEAD - 1 + BACK[b][1]) * 128, 768)]
                for b in range(4)
            ]
            product = jnp.dot(bk[a], jnp.concatenate(parts, axis=0), preferred_element_type=F32)
            total = product if total is None else total + product
        return total

    def outer(ci, _):
        igb[0, :, lanes(ci * 768, 768)] = back(0, ((3, 0, 0),), ci).astype(BF)
        igb[1, :, lanes(ci * 768, 768)] = back(3, ((0, 1, 1),), ci).astype(BF)
        return 0

    lax.fori_loop(0, 3, outer, 0)
    body = pl.ds(128, WIDE)
    far_parts = []
    for g in range(4):
        rows16, at = pl.ds(16 * g, 16), 0 if g == 0 else 7 + g
        far_parts.append(
            remote(igb.at[core, rows16, body], rx.at[0, rows16], bs.at[at], br.at[at], neighbours[0])
        )
    bsends = [
        far_parts[0],
        remote(igb.at[other, :, body], rx.at[1], bs.at[1], br.at[1], neighbours[1]),
    ]
    for copy in far_parts[:EARLY] + bsends[1:]:
        copy.start()

    def inner(ci, _):
        igf[0, :, lanes(ci * 768, 768)] = back(1, ((1, 0, 0), (2, 1, 0), (3, 0, 1)), ci)
        igf[1, :, lanes(ci * 768, 768)] = back(2, ((1, 0, 1), (2, 1, 1), (0, 1, 0)), ci)
        return 0

    lax.fori_loop(0, 3, inner, 0)
    igy[0] = igf[:, :, 0:128].astype(BF)
    igy[1] = igf[:, :, HALO - 128:].astype(BF)
    for k in range(2):
        bsends.append(remote(igy.at[k], ry.at[k], bs.at[2 + k], br.at[2 + k], neighbours[2 + k]))
    for index, m in ((0, core), (1, other)):
        for k, part_lanes in enumerate((low, high)):
            at = 4 + 2 * index + k
            bsends.append(remote(igb.at[m, :, part_lanes], rc.at[index, k], bs.at[at], br.at[at], neighbours[at]))
    for copy in bsends[2:]:
        copy.start()

    mine = 4 * x + y
    remote(w_bf.at[pl.ds(0, 240)].reshape(15, 16, 256), rs_in.at[pl.ds(1, 15)], ws.at[1], wr.at[1], neighbours[1]).wait_recv()
    total = w_s[core, pl.ds(pl.multiple_of(16 * mine, 16), 16)]
    for i in range(1, 16):
        total = total + rs_in[i].astype(F32)
    part[...] = total.astype(BF)
    z_in[z] = total.astype(BF)
    gather_z = [remote(part, z_in.at[z], ws.at[2], wr.at[2], z_peer(i)) for i in (2, 1, 3)]
    for copy in gather_z + far_parts[EARLY:3]:
        copy.start()
    for k, (p, m) in enumerate(blocks):

        def turn_act(i, _, k=k, p=p, m=m):
            q, h = i // 2, lax.rem(i, 2)
            value = swap16(actn[k, q, h, 0:256]).astype(BF)
            for s in range(2):
                act_ref[4 * p + 2 * q + s, pl.ds(16 * h, 16), m] = value[:, 128 * s:128 * s + 128].reshape(16, ROWS, 128)
            return 0

        lax.fori_loop(0, 4, turn_act, 0)

    three = z_in.at[pl.ds(0, 3)]
    remote(three, three, ws.at[2], wr.at[2], neighbours[1]).wait_recv()
    wide = [z_in[i].astype(F32) for i in range(4)]
    total = (wide[0] + wide[1]) + (wide[2] + wide[3])
    fin[core, pl.ds(pl.multiple_of(16 * mine, 16), 16)] = (total * (0.5 * scaling)).astype(BF)
    spread = []
    shard = fin.at[core, pl.ds(pl.multiple_of(16 * mine, 16), 16)]
    for _, peer in plane:
        spread.append(remote(shard, shard, ws.at[3], wr.at[3], peer))
        spread.append(remote(shard, shard, ws.at[4], wr.at[4], twin(peer)))
    spread.append(remote(shard, shard, ws.at[4], wr.at[4], neighbours[1]))
    for copy in spread + far_parts[3:]:
        copy.start()

    def add(index, k, src, m, keep):
        place = (128, ROWS * 128)[k]

        @pl.when(keep)
        def _():
            igf[m, :, pl.ds(place, 128)] = igf[m, :, pl.ds(place, 128)] + src().astype(F32)

    bsends[2].wait_recv()
    bsends[3].wait_recv()
    for m in range(2):
        add(2, 1, lambda m=m: ry[0, m], m, jnp.logical_not(last_y))
        add(3, 0, lambda m=m: ry[1, m], m, jnp.logical_not(first_y))
    for index, m in ((1, other), (0, core)):
        ok = jnp.logical_not(no_far) if index == 0 else True
        for copy in far_parts if index == 0 else [bsends[1]]:
            copy.wait_recv()
        bsends[4 + 2 * index].wait_recv()
        bsends[5 + 2 * index].wait_recv()

        def add_face(index=index, m=m):
            igf[m, :, body] = igf[m, :, body] + rx[index].astype(F32)

        if index == 0:
            pl.when(ok)(add_face)
        else:
            add_face()
        add(4, 1, lambda index=index: rc[index, 0], m, jnp.logical_and(ok, jnp.logical_not(last_y)))
        add(5, 0, lambda index=index: rc[index, 1], m, jnp.logical_and(ok, jnp.logical_not(first_y)))
        for group in (0, 2):
            halves = [
                jnp.concatenate(
                    [igf[m, 16 * g:16 * g + 16, 128 * (n + 1):128 * (n + 2)].astype(BF) for n in range(ROWS)], axis=0
                )
                for g in (group, group + 1)
            ]
            value = swap16(jnp.concatenate(halves, axis=1)).astype(BF)
            for g in range(2):
                at = 16 * (group + g)
                igo[at:at + 16, m] = value[:, 128 * g:128 * g + 128].reshape(16, ROWS, 128)
    remote(w_bf.at[pl.ds(0, 240)], fin.at[core, pl.ds(0, 240)], ws.at[3], wr.at[3], neighbours[1]).wait_recv()
    whole = remote(fin.at[core], fin.at[core], ws.at[4], wr.at[4], neighbours[1])
    whole.wait_recv()
    for copy in sends + bsends + far_parts[1:] + [swap, whole]:
        copy.wait_send()
    remote(three, three, ws.at[2], wr.at[2], neighbours[1]).wait_send()
    remote(w_bf.at[pl.ds(0, 240)], fin.at[core, pl.ds(0, 240)], ws.at[1], wr.at[1], neighbours[1]).wait_send()
    remote(w_bf.at[pl.ds(0, 240)], fin.at[core, pl.ds(0, 240)], ws.at[3], wr.at[3], neighbours[1]).wait_send()


def write_kernel(act, ig, fin, act_ref, ig_ref, wg_ref, wgo, sem):
    copies = [
        pltpu.make_async_copy(act.at[pl.ds(2 * i, 2)], act_ref.at[pl.ds(2 * i, 2)], sem.at[i])
        for i in range(4)
    ]
    copies.append(pltpu.make_async_copy(ig, ig_ref, sem.at[4]))
    for copy in copies:
        copy.start()
    for p in range(2):
        for q in range(2):
            taps = [(a, b) for a in (3 - p, 1 - p) for b in (3 - q, 1 - q)]
            for i, (a, b) in enumerate(taps):
                value = fin[p, 128 * q:128 * q + 128, 64 * i:64 * i + 64]
                wgo[a, b] = value.astype(F32).reshape(4, 32, 64)
    copies.append(pltpu.make_async_copy(wgo, wg_ref, sem.at[5]))
    copies[-1].start()
    for copy in copies:
        copy.wait()


def on_device(volume, kernel, cotangent):
    cells = volume.shape[1] * volume.shape[2] * volume.shape[3]
    scaling = 1.0 / math.sqrt(cells * lax.axis_size("gx") * lax.axis_size("gy"))
    anywhere = pl.BlockSpec(memory_space=pltpu.HBM)
    inside = pl.BlockSpec(memory_space=pltpu.VMEM)
    dma = pltpu.SemaphoreType.DMA
    operands = [
        pltpu.with_memory_space_constraint(value, pltpu.HBM)
        for value in (volume, kernel, cotangent.reshape(8, 32, 2, ROWS, 128))
    ]
    results = pl.pallas_call(
        functools.partial(step_kernel, scaling),
        out_shape=(
            pltpu.VMEM((8, 32, 2, ROWS, 128), BF),
            pltpu.VMEM((64, 2, ROWS, 128), BF),
            pltpu.VMEM((2, 256, 256), BF),
        ),
        in_specs=[anywhere, anywhere, anywhere],
        out_specs=(inside, inside, inside),
        scratch_shapes=[
            pltpu.VMEM((64, 2, ROWS, 128), BF),
            pltpu.VMEM((4, 4, 4, 32, 64), BF),
            pltpu.VMEM((2, 64, ROWS, 128), BF),
            pltpu.VMEM((256, 256), BF),
            pltpu.VMEM((4, 64, HALO), BF),
            pltpu.VMEM((4, 4, 32, ROWS, 128), BF),
            pltpu.VMEM((4, 2, 2, 256, 256), F32),
            pltpu.VMEM((4, 2, 2, 16 + 256, 256), BF),
            pltpu.VMEM((2, 2, 256, 512), F32),
            pltpu.VMEM((2, 2, 2, 128, (LEAD + ROWS + 3) * 128), BF),
            pltpu.VMEM((2, 256, 256), BF),
            pltpu.VMEM((4, 64, 512), BF),
            pltpu.VMEM((2, 256, 256), F32),
            pltpu.VMEM((256, 256), BF),
            pltpu.VMEM((256, 256), BF),
            pltpu.VMEM((256, 256), BF),
            pltpu.VMEM((16, 16, 256), BF),
            pltpu.VMEM((16, 256), BF),
            pltpu.VMEM((4, 16, 256), BF),
            pltpu.VMEM((2, 64, HALO), F32),
            pltpu.VMEM((2, 64, HALO), BF),
            pltpu.VMEM((2, 2, 64, 128), BF),
            pltpu.VMEM((2, 64, WIDE), BF),
            pltpu.VMEM((2, 2, 64, 128), BF),
            pltpu.VMEM((2, 2, 64, 128), BF),
            dma((6,)), dma((8,)), dma((8,)), dma((11,)), dma((11,)), dma((5,)), dma((5,)),
        ],
        compiler_params=pltpu.CompilerParams(
            collective_id=0, has_side_effects=True, vmem_limit_bytes=40 * 1024 * 1024
        ),
        name="conv_step",
    )(*operands)
    results = [pltpu.with_memory_space_constraint(value, pltpu.VMEM) for value in results]
    act, ig, wg = pl.pallas_call(
        write_kernel,
        out_shape=(
            jax.ShapeDtypeStruct((8, 32, 2, ROWS, 128), BF),
            jax.ShapeDtypeStruct((64, 2, ROWS, 128), BF),
            jax.ShapeDtypeStruct((4, 4, 4, 32, 64), F32),
        ),
        in_specs=[inside] * 3,
        out_specs=(anywhere,) * 3,
        scratch_shapes=[pltpu.VMEM((4, 4, 4, 32, 64), F32), dma((6,))],
        compiler_params=pltpu.CompilerParams(vmem_limit_bytes=16 * 1024 * 1024),
        name="write_out",
    )(*results)
    return act.reshape(2, 2, 2, 32, 2, ROWS, 128), ig, wg


def solution(mesh):
    placed = (P(None, "gx", "gy", None), P(), P(None, None, None, None, "gx", "gy", None))
    return jax.shard_map(
        on_device,
        mesh=mesh,
        in_specs=placed,
        out_specs=(P(None, None, None, None, "gx", "gy", None), P(None, "gx", "gy", None), P()),
        check_vma=False,
    )
```

```python
import functools
import math

import jax
import jax.numpy as jnp
from jax import lax
from jax.experimental import pallas as pl
from jax.experimental.pallas import tpu as pltpu
from jax.sharding import PartitionSpec as P

BF = jnp.bfloat16
F32 = jnp.float32
MESH = pl.DeviceIdType.MESH
BACK = ((1, -1), (0, 0), (1, 0), (0, 1))
ROWS = 16
WIDE = ROWS * 128
HALO = (ROWS + 2) * 128
EARLY = 2
LEAD = 8


def remote(src, dst, send, recv, device):
    return pltpu.make_async_remote_copy(
        src_ref=src, dst_ref=dst, send_sem=send, recv_sem=recv,
        device_id=device, device_id_type=MESH,
    )


def nt_dot(a, b):
    return lax.dot_general(a, b, (((1,), (1,)), ((), ())), preferred_element_type=F32)


def lanes(start, size):
    return pl.ds(pl.multiple_of(start, 128), size)


def step_kernel(
    scaling, vol_ref, ker_hbm, cot_ref, act_ref, igo, fin,
    volb, ker_ref, face, swap_rows, vt, cotb, cotn, actn, u_s, g_s, ak, bk, w_s,
    w_send, w_recv, w_bf, rs_in, part, z_in,
    igf, igb, igy, rx, ry, rc,
    l_sem, fs, fr, bs, br, ws, wr,
):
    gx, gy = lax.axis_index("gx"), lax.axis_index("gy")
    core = lax.rem(gx, 2)
    x, z_hi = gx // 4, lax.rem(gx // 2, 2)
    z_lo, y = gy // 4, lax.rem(gy, 4)
    z = 2 * z_hi + z_lo
    other = 1 - core
    far_gx = lax.rem(gx + 15 + 2 * core, 16)
    sib_gx = gx + 1 - 2 * core
    low_gy, high_gy = lax.rem(gy + 7, 8), lax.rem(gy + 1, 8)
    first_y, last_y = gy == 0, gy == 7
    no_far = jnp.logical_or(gx == 0, gx == 15)

    def plane_peer(i):
        px, py = lax.rem(x + i // 4, 4), lax.rem(y + i % 4, 4)
        return px * 4 + py, (px * 4 + 2 * z_hi + core, 4 * z_lo + py)

    def z_peer(i):
        pz = lax.rem(z + i, 4)
        return (4 * x + 2 * (pz // 2) + core, 4 * lax.rem(pz, 2) + y)

    neighbours = [
        (far_gx, gy), (sib_gx, gy), (gx, low_gy), (gx, high_gy),
        (far_gx, low_gy), (far_gx, high_gy), (sib_gx, low_gy), (sib_gx, high_gy),
    ]
    order = sorted(range(1, 16), key=lambda i: -(min(i // 4, 4 - i // 4) + min(i % 4, 4 - i % 4)))

    def twin(device):
        return (device[0] + 1 - 2 * core, device[1])

    plane = [plane_peer(i) for i in order]
    peers = neighbours + [d for _, d in plane] + [twin(d) for _, d in plane] + [z_peer(i) for i in range(1, 4)]

    vol_copy = pltpu.make_async_copy(vol_ref, volb, l_sem.at[4])
    vol_copy.start()
    ker_copy = pltpu.make_async_copy(ker_hbm, ker_ref, l_sem.at[5])
    ker_copy.start()
    blocks = [(1, 0), (0, 1), (other, other), (core, core)]
    cot_copies = []
    for k, (p, m) in enumerate(blocks):
        copy = pltpu.make_async_copy(
            cot_ref.at[pl.ds(4 * p, 4), :, m], cotb.at[k], l_sem.at[k]
        )
        copy.start()
        cot_copies.append(copy)

    barrier = pltpu.get_barrier_semaphore()
    for peer in peers:
        pl.semaphore_signal(barrier, inc=1, device_id=peer, device_id_type=MESH)

    down_i = lax.broadcasted_iota(jnp.int32, (256, 256), 0)
    along = lax.broadcasted_iota(jnp.int32, (256, 256), 1)
    swapped = jnp.bitwise_or(jnp.left_shift(jnp.bitwise_and(along, 15), 4), jnp.right_shift(along, 4))
    swap_rows[...] = jnp.where(down_i == swapped, 1.0, 0.0).astype(BF)

    def swap16(value):
        return jnp.dot(swap_rows[...], value, preferred_element_type=F32)

    def turn_in(left, right, put_left, put_right):
        both = swap16(jnp.concatenate([left.reshape(256, 128), right.reshape(256, 128)], axis=1)).astype(BF)
        for n in range(ROWS):
            put_left(n, both[16 * n:16 * n + 16, 0:128])
            put_right(n, both[16 * n:16 * n + 16, 128:256])

    def into(slot, group):
        def put(n, value):
            vt[slot, 16 * group:16 * group + 16, 128 * (n + 1):128 * (n + 2)] = value

        return put

    vol_copy.wait()
    for group in range(4):
        rows16 = slice(16 * group, 16 * group + 16)
        turn_in(volb[rows16, 0], volb[rows16, 1], into(1, group), into(2, group))
    pl.semaphore_wait(barrier, len(peers))

    sends = [
        remote(volb.at[:, core], face.at[0], fs.at[0], fr.at[0], neighbours[0]),
        remote(volb.at[:, other], face.at[1], fs.at[1], fr.at[1], neighbours[1]),
    ]
    first, last = pl.ds(128, 128), pl.ds(ROWS * 128, 128)
    low, high = pl.ds(0, 128), pl.ds((ROWS + 1) * 128, 128)
    own = pl.ds(1, 2)
    ysends = [
        remote(vt.at[own, :, first], vt.at[own, :, high], fs.at[2], fr.at[2], neighbours[2]),
        remote(vt.at[own, :, last], vt.at[own, :, low], fs.at[3], fr.at[3], neighbours[3]),
    ]
    for k, (m, slot) in enumerate(((core, 3 - 3 * core), (other, 3 * core))):
        base = 4 + 2 * k
        ysends.append(remote(vt.at[1 + m, :, first], vt.at[slot, :, high], fs.at[base], fr.at[base], neighbours[base]))
        ysends.append(remote(vt.at[1 + m, :, last], vt.at[slot, :, low], fs.at[base + 1], fr.at[base + 1], neighbours[base + 1]))
    for copy in ysends[:2] + sends + ysends[2:]:
        copy.start()
    sends += ysends

    half = jnp.asarray(0.5, BF)
    ker_copy.wait()
    for p in range(2):
        for q in range(2):
            pieces = [
                ker_ref[a, b].reshape(128, 64)
                for a in (3 - p, 1 - p)
                for b in (3 - q, 1 - q)
            ]
            ak[p, 128 * q:128 * q + 128] = jnp.concatenate(pieces, axis=1) * half
    for a in range(4):
        bk[a] = ker_ref[a].reshape(512, 64).astype(F32).T.astype(BF) * half
    w_s[...] = jnp.zeros((2, 256, 256), F32)
    for at, count in ((LEAD - 4, 5), (LEAD + ROWS, 2)):
        g_s[:, :, :, :, 128 * at:128 * (at + count)] = jnp.zeros((2, 2, 2, 128, 128 * count), BF)

    lane = lax.broadcasted_iota(jnp.int32, (32, 128), 1)

    def up(u):
        return jnp.where(lane == 0, 0.0, pltpu.roll(u, 1, axis=1))

    def down(u):
        return jnp.where(lane == 127, 0.0, pltpu.roll(u, 127, axis=1))

    def group(members, weights, low_x, w_at, between=None):
        def tile(start, size):
            return jnp.concatenate(
                [
                    vt[low_x + i, :, lanes(start + 128 * j, size)]
                    for i in range(2)
                    for j in range(2)
                ],
                axis=0,
            )

        def product(start, slot):
            u = jnp.dot(weights(), tile(start, 512), preferred_element_type=F32)
            u_s[slot, 0:len(members)] = u.reshape(len(members), 256, 512)

        def grad(first, size):
            rows = [
                g_s[p, q, m, :, lanes((first - q + LEAD) * 128, size)]
                for _, p, m in members
                for q in range(2)
            ]
            value = nt_dot(jnp.concatenate(rows, axis=0), tile(128 * (jnp.maximum(first, 1) if size == 512 else first), size))
            w_s[w_at] += value.reshape(len(members), 256, 256)

        def finish(first, slot, corners, sides):
            for member, (k, p, m) in enumerate(members):
                for j in range(corners):
                    for q in sides:
                        n = first + j - q
                        if j == 3 and q == 0:
                            outside = n == ROWS
                            put = n
                            place = jnp.where(outside, LEAD + ROWS + 2, n + LEAD)
                            take = jnp.minimum(n, ROWS - 1)
                        else:
                            put, place, take = n, n + LEAD, n
                        put = pl.ds(pl.multiple_of(16 * put, 16), 16)
                        take = pl.ds(pl.multiple_of(16 * take, 16), 16)
                        taps = [
                            u_s[slot, member, 128 * q + 32 * c:128 * q + 32 * c + 32, 128 * j:128 * j + 128]
                            for c in range(4)
                        ]
                        halves = (taps[1] + up(taps[3]), taps[2] + down(taps[0]))
                        grads = []
                        for s in range(2):
                            t_h = jnp.tanh(halves[s])
                            w = 1.0 + t_h
                            act = halves[s] * w
                            slope = w + act * (1.0 - t_h)
                            at = slice(128 * s, 128 * s + 128)
                            act = act.astype(BF)
                            for h in range(2):
                                actn[k, q, h, put, at] = act[16 * h:16 * h + 16]
                            cot = jnp.concatenate([cotn[k, q, h, take, at] for h in range(2)], axis=0)
                            grads.append((cot * slope).astype(BF))
                        four = (
                            jnp.where(lane == 0, jnp.zeros((), BF), pltpu.roll(grads[1], 1, axis=1)),
                            grads[0],
                            grads[1],
                            jnp.where(lane == 127, jnp.zeros((), BF), pltpu.roll(grads[0], 127, axis=1)),
                        )
                        g_s[p, q, m, :, lanes(place * 128, 128)] = jnp.concatenate(four, axis=0)

        product(128, 0)

        def step(t, _):
            now = lax.rem(t, 2)
            grad(4 * t - 3, 512)
            finish(4 * t + 1, now, 4, (0, 1))
            product(jnp.where(t == 3, 0, 512 * t + 640), 1 - now)
            return 0

        if between is None:
            lax.fori_loop(0, 4, step, 0)
        else:
            lax.fori_loop(0, 2, step, 0)
            between()
            lax.fori_loop(2, 4, step, 0)
        grad(13, 512)
        finish(0, 0, 1, (0,))
        grad(0, 128)

    for copy in cot_copies:
        copy.wait()

    def turn_cot(i, _):
        k, q, h = i // 4, lax.rem(i // 2, 2), lax.rem(i, 2)
        pair = [
            cotb[k, 2 * q + s, pl.ds(16 * h, 16)].reshape(256, 128) for s in range(2)
        ]
        cotn[k, q, h] = swap16(jnp.concatenate(pair, axis=1))
        return 0

    lax.fori_loop(0, 16, turn_cot, 0)

    def y_rows():
        ysends[0].wait_recv()
        ysends[1].wait_recv()

        @pl.when(first_y)
        def _():
            vt[own, :, low] = jnp.zeros((2, 64, 128), BF)

        @pl.when(last_y)
        def _():
            vt[own, :, high] = jnp.zeros((2, 64, 128), BF)

    group(
        [(1, 0, 1), (0, 1, 0)], lambda: ak[...].reshape(512, 256), 1, slice(0, 2), y_rows
    )

    def halo(index, slot):
        sends[index].wait_recv()
        for group in (0, 2):
            turn_in(
                face[index, 16 * group:16 * group + 16],
                face[index, 16 * group + 16:16 * group + 32],
                into(slot, group), into(slot, group + 1),
            )
        sends[4 + 2 * index].wait_recv()
        sends[5 + 2 * index].wait_recv()

        @pl.when(first_y)
        def _():
            vt[slot, :, low] = jnp.zeros((64, 128), BF)

        @pl.when(last_y)
        def _():
            vt[slot, :, high] = jnp.zeros((64, 128), BF)

    halo(1, 3 - 3 * core)
    group([(2, other, other)], lambda: ak[other], 2 * other, pl.ds(other, 1))
    w_send[...] = w_s[other].astype(BF)
    swap = remote(w_send, w_recv, ws.at[0], wr.at[0], neighbours[1])
    swap.start()

    halo(0, 3 * core)

    @pl.when(no_far)
    def _():
        vt[3 * core] = jnp.zeros((64, HALO), BF)

    group([(3, core, core)], lambda: ak[core], 2 * core, pl.ds(core, 1))

    swap.wait_recv()
    w_s[core] = w_s[core] + w_recv[...].astype(F32)
    w_bf[...] = w_s[core].astype(BF)
    scatter = []
    for i, (index, peer) in zip(order, plane):
        scatter.append(remote(w_bf.at[pl.ds(pl.multiple_of(16 * index, 16), 16)], rs_in.at[i], ws.at[1], wr.at[1], peer))
    for copy in scatter:
        copy.start()

    def back(target, terms, ci):
        total = None
        for a, p, m in terms:
            parts = [
                g_s[p, BACK[b][0], m, :, lanes((ci * 6 + LEAD - 1 + BACK[b][1]) * 128, 768)]
                for b in range(4)
            ]
            product = jnp.dot(bk[a], jnp.concatenate(parts, axis=0), preferred_element_type=F32)
            total = product if total is None else total + product
        return total

    def outer(ci, _):
        igb[0, :, lanes(ci * 768, 768)] = back(0, ((3, 0, 0),), ci).astype(BF)
        igb[1, :, lanes(ci * 768, 768)] = back(3, ((0, 1, 1),), ci).astype(BF)
        return 0

    lax.fori_loop(0, 3, outer, 0)
    body = pl.ds(128, WIDE)
    far_parts = []
    for g in range(4):
        rows16, at = pl.ds(16 * g, 16), 0 if g == 0 else 7 + g
        far_parts.append(
            remote(igb.at[core, rows16, body], rx.at[0, rows16], bs.at[at], br.at[at], neighbours[0])
        )
    bsends = [
        far_parts[0],
        remote(igb.at[other, :, body], rx.at[1], bs.at[1], br.at[1], neighbours[1]),
    ]
    for copy in far_parts[:EARLY] + bsends[1:]:
        copy.start()

    def inner(ci, _):
        igf[0, :, lanes(ci * 768, 768)] = back(1, ((1, 0, 0), (2, 1, 0), (3, 0, 1)), ci)
        igf[1, :, lanes(ci * 768, 768)] = back(2, ((1, 0, 1), (2, 1, 1), (0, 1, 0)), ci)
        return 0

    lax.fori_loop(0, 3, inner, 0)
    igy[0] = igf[:, :, 0:128].astype(BF)
    igy[1] = igf[:, :, HALO - 128:].astype(BF)
    for k in range(2):
        bsends.append(remote(igy.at[k], ry.at[k], bs.at[2 + k], br.at[2 + k], neighbours[2 + k]))
    for index, m in ((0, core), (1, other)):
        for k, part_lanes in enumerate((low, high)):
            at = 4 + 2 * index + k
            bsends.append(remote(igb.at[m, :, part_lanes], rc.at[index, k], bs.at[at], br.at[at], neighbours[at]))
    for copy in bsends[2:]:
        copy.start()

    mine = 4 * x + y
    remote(w_bf.at[pl.ds(0, 240)].reshape(15, 16, 256), rs_in.at[pl.ds(1, 15)], ws.at[1], wr.at[1], neighbours[1]).wait_recv()
    total = w_s[core, pl.ds(pl.multiple_of(16 * mine, 16), 16)]
    for i in range(1, 16):
        total = total + rs_in[i].astype(F32)
    part[...] = total.astype(BF)
    z_in[z] = total.astype(BF)
    gather_z = [remote(part, z_in.at[z], ws.at[2], wr.at[2], z_peer(i)) for i in (2, 1, 3)]
    for copy in gather_z + far_parts[EARLY:3]:
        copy.start()
    for k, (p, m) in enumerate(blocks):

        def turn_act(i, _, k=k, p=p, m=m):
            q, h = i // 2, lax.rem(i, 2)
            value = swap16(actn[k, q, h, 0:256]).astype(BF)
            for s in range(2):
                act_ref[4 * p + 2 * q + s, pl.ds(16 * h, 16), m] = value[:, 128 * s:128 * s + 128].reshape(16, ROWS, 128)
            return 0

        lax.fori_loop(0, 4, turn_act, 0)

    three = z_in.at[pl.ds(0, 3)]
    remote(three, three, ws.at[2], wr.at[2], neighbours[1]).wait_recv()
    wide = [z_in[i].astype(F32) for i in range(4)]
    total = (wide[0] + wide[1]) + (wide[2] + wide[3])
    fin[core, pl.ds(pl.multiple_of(16 * mine, 16), 16)] = (total * (0.5 * scaling)).astype(BF)
    spread = []
    shard = fin.at[core, pl.ds(pl.multiple_of(16 * mine, 16), 16)]
    for _, peer in plane:
        spread.append(remote(shard, shard, ws.at[3], wr.at[3], peer))
        spread.append(remote(shard, shard, ws.at[4], wr.at[4], twin(peer)))
    spread.append(remote(shard, shard, ws.at[4], wr.at[4], neighbours[1]))
    for copy in spread + far_parts[3:]:
        copy.start()

    def add(index, k, src, m, keep):
        place = (128, ROWS * 128)[k]

        @pl.when(keep)
        def _():
            igf[m, :, pl.ds(place, 128)] = igf[m, :, pl.ds(place, 128)] + src().astype(F32)

    bsends[2].wait_recv()
    bsends[3].wait_recv()
    for m in range(2):
        add(2, 1, lambda m=m: ry[0, m], m, jnp.logical_not(last_y))
        add(3, 0, lambda m=m: ry[1, m], m, jnp.logical_not(first_y))
    for index, m in ((1, other), (0, core)):
        ok = jnp.logical_not(no_far) if index == 0 else True
        for copy in far_parts if index == 0 else [bsends[1]]:
            copy.wait_recv()
        bsends[4 + 2 * index].wait_recv()
        bsends[5 + 2 * index].wait_recv()

        def add_face(index=index, m=m):
            igf[m, :, body] = igf[m, :, body] + rx[index].astype(F32)

        if index == 0:
            pl.when(ok)(add_face)
        else:
            add_face()
        add(4, 1, lambda index=index: rc[index, 0], m, jnp.logical_and(ok, jnp.logical_not(last_y)))
        add(5, 0, lambda index=index: rc[index, 1], m, jnp.logical_and(ok, jnp.logical_not(first_y)))
        for group in (0, 2):
            halves = [
                jnp.concatenate(
                    [igf[m, 16 * g:16 * g + 16, 128 * (n + 1):128 * (n + 2)].astype(BF) for n in range(ROWS)], axis=0
                )
                for g in (group, group + 1)
            ]
            value = swap16(jnp.concatenate(halves, axis=1)).astype(BF)
            for g in range(2):
                at = 16 * (group + g)
                igo[at:at + 16, m] = value[:, 128 * g:128 * g + 128].reshape(16, ROWS, 128)
    remote(w_bf.at[pl.ds(0, 240)], fin.at[core, pl.ds(0, 240)], ws.at[3], wr.at[3], neighbours[1]).wait_recv()
    whole = remote(fin.at[core], fin.at[core], ws.at[4], wr.at[4], neighbours[1])
    whole.wait_recv()
    for copy in sends + bsends + far_parts[1:] + [swap, whole]:
        copy.wait_send()
    remote(three, three, ws.at[2], wr.at[2], neighbours[1]).wait_send()
    remote(w_bf.at[pl.ds(0, 240)], fin.at[core, pl.ds(0, 240)], ws.at[1], wr.at[1], neighbours[1]).wait_send()
    remote(w_bf.at[pl.ds(0, 240)], fin.at[core, pl.ds(0, 240)], ws.at[3], wr.at[3], neighbours[1]).wait_send()


def write_kernel(act, ig, fin, act_ref, ig_ref, wg_ref, wgo, sem):
    copies = [
        pltpu.make_async_copy(act.at[pl.ds(2 * i, 2)], act_ref.at[pl.ds(2 * i, 2)], sem.at[i])
        for i in range(4)
    ]
    copies.append(pltpu.make_async_copy(ig, ig_ref, sem.at[4]))
    for copy in copies:
        copy.start()
    for p in range(2):
        for q in range(2):
            taps = [(a, b) for a in (3 - p, 1 - p) for b in (3 - q, 1 - q)]
            for i, (a, b) in enumerate(taps):
                value = fin[p, 128 * q:128 * q + 128, 64 * i:64 * i + 64]
                wgo[a, b] = value.astype(F32).reshape(4, 32, 64)
    copies.append(pltpu.make_async_copy(wgo, wg_ref, sem.at[5]))
    copies[-1].start()
    for copy in copies:
        copy.wait()


def on_device(volume, kernel, cotangent):
    cells = volume.shape[1] * volume.shape[2] * volume.shape[3]
    scaling = 1.0 / math.sqrt(cells * lax.axis_size("gx") * lax.axis_size("gy"))
    anywhere = pl.BlockSpec(memory_space=pltpu.HBM)
    inside = pl.BlockSpec(memory_space=pltpu.VMEM)
    dma = pltpu.SemaphoreType.DMA
    operands = [
        pltpu.with_memory_space_constraint(value, pltpu.HBM)
        for value in (volume, kernel, cotangent.reshape(8, 32, 2, ROWS, 128))
    ]
    results = pl.pallas_call(
        functools.partial(step_kernel, scaling),
        out_shape=(
            pltpu.VMEM((8, 32, 2, ROWS, 128), BF),
            pltpu.VMEM((64, 2, ROWS, 128), BF),
            pltpu.VMEM((2, 256, 256), BF),
        ),
        in_specs=[anywhere, anywhere, anywhere],
        out_specs=(inside, inside, inside),
        scratch_shapes=[
            pltpu.VMEM((64, 2, ROWS, 128), BF),
            pltpu.VMEM((4, 4, 4, 32, 64), BF),
            pltpu.VMEM((2, 64, ROWS, 128), BF),
            pltpu.VMEM((256, 256), BF),
            pltpu.VMEM((4, 64, HALO), BF),
            pltpu.VMEM((4, 4, 32, ROWS, 128), BF),
            pltpu.VMEM((4, 2, 2, 256, 256), F32),
            pltpu.VMEM((4, 2, 2, 16 + 256, 256), BF),
            pltpu.VMEM((2, 2, 256, 512), F32),
            pltpu.VMEM((2, 2, 2, 128, (LEAD + ROWS + 3) * 128), BF),
            pltpu.VMEM((2, 256, 256), BF),
            pltpu.VMEM((4, 64, 512), BF),
            pltpu.VMEM((2, 256, 256), F32),
            pltpu.VMEM((256, 256), BF),
            pltpu.VMEM((256, 256), BF),
            pltpu.VMEM((256, 256), BF),
            pltpu.VMEM((16, 16, 256), BF),
            pltpu.VMEM((16, 256), BF),
            pltpu.VMEM((4, 16, 256), BF),
            pltpu.VMEM((2, 64, HALO), F32),
            pltpu.VMEM((2, 64, HALO), BF),
            pltpu.VMEM((2, 2, 64, 128), BF),
            pltpu.VMEM((2, 64, WIDE), BF),
            pltpu.VMEM((2, 2, 64, 128), BF),
            pltpu.VMEM((2, 2, 64, 128), BF),
            dma((6,)), dma((8,)), dma((8,)), dma((11,)), dma((11,)), dma((5,)), dma((5,)),
        ],
        compiler_params=pltpu.CompilerParams(
            collective_id=0, has_side_effects=True, vmem_limit_bytes=40 * 1024 * 1024
        ),
        name="conv_step",
    )(*operands)
    results = [pltpu.with_memory_space_constraint(value, pltpu.VMEM) for value in results]
    act, ig, wg = pl.pallas_call(
        write_kernel,
        out_shape=(
            jax.ShapeDtypeStruct((8, 32, 2, ROWS, 128), BF),
            jax.ShapeDtypeStruct((64, 2, ROWS, 128), BF),
            jax.ShapeDtypeStruct((4, 4, 4, 32, 64), F32),
        ),
        in_specs=[inside] * 3,
        out_specs=(anywhere,) * 3,
        scratch_shapes=[pltpu.VMEM((4, 4, 4, 32, 64), F32), dma((6,))],
        compiler_params=pltpu.CompilerParams(vmem_limit_bytes=16 * 1024 * 1024),
        name="write_out",
    )(*results)
    return act.reshape(2, 2, 2, 32, 2, ROWS, 128), ig, wg


def solution(mesh):
    placed = (P(None, "gx", "gy", None), P(), P(None, None, None, None, "gx", "gy", None))
    return jax.shard_map(
        on_device,
        mesh=mesh,
        in_specs=placed,
        out_specs=(P(None, None, None, None, "gx", "gy", None), P(None, "gx", "gy", None), P()),
        check_vma=False,
    )
```
